256 devices in a mesh: ang: 16 (over y_hi, x, core), row: 16 (over z, y_lo).
Axes of the slice: x: 4, y: 4 (y_hi: 2, y_lo: 2; y = y_hi * 2 + y_lo), z: 8, core: 2. Of those that a mesh axis runs over, the one named last changes fastest.
Arguments:
- dual_field: bfloat16 [64, 32, 2048], P('ang', 'row'), may hold values from -2 to 3
- forward: bfloat16 [64, 32, 2048], P('ang', 'row'), may hold values from -2 to 3
- sinogram: bfloat16 [64, 32, 2048], P('ang', 'row'), may hold values from -2 to 3
- first_weight: bfloat16 [3, 3, 32, 3], replicated, may hold values from -1.25 to 1.25
- first_bias: float32 [32], replicated, may hold values from -3 to 3
- middle_weight: bfloat16 [3, 3, 32, 32], replicated, may hold values from -0.375 to 0.375
- middle_bias: float32 [32], replicated, may hold values from -3 to 3
- last_weight: bfloat16 [3, 3, 1, 32], replicated, may hold values from -0.1875 to 0.1875
- magnify: float32 [64], P('ang'), may hold values from 0.85 to 0.95
- detector_shift: float32 [64], P('ang'), may hold values from -8 to 8
- row_fraction: float32 [64], P('ang'), may hold values from 0 to 1
- offsets: int32 [16, 64], replicated, may hold values from 0 to 27, as said below
- slab_order: int32 [64], replicated, may hold values from 0 to 63, each once
Outputs:
- new_dual: bfloat16 [64, 32, 2048], P('ang', 'row')
- volume: float32 [256, 2048], P('row', 'ang')
The draws below stay inside these ranges and needn't reach their ends.
Inputs may be any that keep to these rules, and one draw needn't show every extreme that they name: offsets[b, q] lies within 2 rows of q * 27 // 63. `slab_order`: each slab appears once.
All inputs are finite; a program needn't handle non-finite values.
Results may differ from the reference program's by a relative error of at most 0.0022.
The reference program's roundings to bfloat16 on the way count: a program that leaves them out, or rounds other values in their place, can miss the bound.
Values may be sent and summed in bfloat16 or wider, within the bound.
No kernel may reach another device: no remote copies, remote signals or barrier semaphores. Data moves between devices by JAX's collectives and lax.ppermute only.
A program may use at most 64 MiB of HBM per device.

```python
import math
import jax
import jax.numpy as jnp
from jax import lax

ANG_DEV = 4
ROWS_DEV = 2
U = 2048
CH = 32
SLAB_Z = 4
ANGLES = 64
R = 32
SLABS = 64
BLOCKS = 16


def profile_field(key, salt):
    folded = jax.random.fold_in(key, salt)
    noise_key, amp_key, shift_key = jax.random.split(folded, 3)
    noise = jnp.clip(0.6 * jax.random.normal(noise_key, (ANGLES, R, U), jnp.float32), -2.0, 2.0)
    amplitude = jax.random.uniform(amp_key, (ANGLES, R, 1), jnp.float32, 0.6, 1.0)
    shift = jax.random.uniform(shift_key, (ANGLES, 1, 1), jnp.float32, -U / 32.0, U / 32.0)
    columns = jnp.arange(U, dtype=jnp.float32)[None, None, :]
    ratio = (columns - (U - 1) / 2.0 - shift) / (U / 4.0)
    profile = amplitude * jnp.sqrt(jnp.maximum(1.0 - ratio * ratio, 0.0))
    return (noise + profile).astype(jnp.bfloat16)


def draw_dual_field(key, part):
    return profile_field(key, 101)


def draw_forward(key, part):
    return profile_field(key, 202)


def draw_sinogram(key, part):
    return profile_field(key, 303)


def draw_offsets(key, part):
    base_rows = jnp.arange(SLABS, dtype=jnp.int32) * (R - SLAB_Z - 1) // (SLABS - 1)
    jitter = jax.random.randint(key, (BLOCKS, SLABS), -ROWS_DEV, ROWS_DEV + 1)
    return jnp.clip(base_rows[None, :] + jitter, 0, R - SLAB_Z - 1).astype(jnp.int32)


def block_levels(stream_key, dims, cuts, least, high):
    level, own = 1.0, jax.random.fold_in(stream_key, 6)
    for axis_at, blocks in cuts:
        draws = jnp.exp(jax.random.uniform(jax.random.fold_in(own, axis_at), (blocks,), jnp.float32, least / len(cuts), high / len(cuts)))
        level = level * jnp.repeat(draws, dims[axis_at] // blocks).reshape([-1 if axis == axis_at else 1 for axis in range(len(dims))])
    return level


def bell_draw(rng, extent, scale, bound, kind=jnp.bfloat16):
    array = scale * jax.random.normal(rng, extent, jnp.float32)
    return jnp.clip(array, min=-bound, max=bound).astype(kind)


def setup_inputs(seed: int = 0) -> dict:
    seeds = jax.random.split(jax.random.key(seed), 14)
    dual_field = draw_dual_field(jax.random.fold_in(seeds[13], 71), 0)
    forward = draw_forward(jax.random.fold_in(seeds[13], 71), 0)
    sinogram = draw_sinogram(jax.random.fold_in(seeds[13], 71), 0)
    first_weight = bell_draw(seeds[3], (3, 3, CH, 3), 27 ** -0.5, 1.25)
    first_bias = bell_draw(seeds[4], (CH,), 0.5, 3.0, jnp.float32)
    middle_weight = bell_draw(seeds[5], (3, 3, CH, CH), (9 * CH) ** -0.5, 0.375)
    middle_bias = bell_draw(seeds[6], (CH,), 0.5, 3.0, jnp.float32)
    last_weight = bell_draw(seeds[7], (3, 3, 1, CH), (36 * CH) ** -0.5, 0.1875)
    magnify = jnp.clip(0.85 + 0.099999964 * jax.random.uniform(seeds[8], (ANGLES,), jnp.float32) ** block_levels(seeds[8], (ANGLES,), ((0, 16),), -0.2, 0.2), 0.85, 0.95)
    detector_shift = jnp.clip(jax.random.uniform(seeds[9], (ANGLES,), jnp.float32, -8.0, 8.0) * block_levels(seeds[9], (ANGLES,), ((0, 16),), -0.4, 0.0), -8.0, 8.0)
    row_fraction = jnp.clip(1.0 * jax.random.uniform(seeds[10], (ANGLES,), jnp.float32) ** block_levels(seeds[10], (ANGLES,), ((0, 16),), -0.2, 0.2), 0.0, 1.0)
    offsets = draw_offsets(jax.random.fold_in(seeds[13], 71), 0)
    slab_order = jax.random.permutation(seeds[12], SLABS).astype(jnp.int32)
    return {"dual_field": dual_field, "forward": forward, "sinogram": sinogram, "first_weight": first_weight, "first_bias": first_bias, "middle_weight": middle_weight, "middle_bias": middle_bias, "last_weight": last_weight, "magnify": magnify, "detector_shift": detector_shift, "row_fraction": row_fraction, "offsets": offsets, "slab_order": slab_order}


def ramp_block(start, width, size):
    row_ids = jnp.arange(size, dtype=jnp.int32)[:, None]
    col_ids = start + jnp.arange(width, dtype=jnp.int32)[None, :]
    offset_odd = jnp.abs(row_ids - col_ids) % 2 == 1
    distance = jnp.where(offset_odd, row_ids - col_ids, 1).astype(jnp.float32)
    kernel = jnp.where(row_ids == col_ids, 0.25, jnp.where(offset_odd, -1.0 / (math.pi * math.pi * distance * distance), 0.0))
    return kernel.astype(jnp.bfloat16)

def conv_taps(inputs, weights):
    length = inputs.shape[1] - 2
    columns = inputs.shape[2]
    padded = jnp.pad(inputs.astype(jnp.float32), ((0, 0), (0, 0), (1, 1)))
    result = jnp.zeros((weights.shape[2], length, columns), jnp.float32)
    for ang_tap in range(3):
        for col_tap in range(3):
            result = result + jnp.einsum('oc,cau->oau', weights[ang_tap, col_tap].astype(jnp.float32), padded[:, ang_tap:ang_tap + length, col_tap:col_tap + columns])
    return result

def wrap_angles(values):
    return jnp.concatenate([values[:, -1:], values, values[:, :1]], axis=1)

def interpolate(filtered, magnify, detector_shift):
    columns = filtered.shape[2]
    centre = (columns - 1) / 2.0
    places = (jnp.arange(columns, dtype=jnp.float32)[None, :] - centre) * magnify[:, None] + centre + detector_shift[:, None]
    floors = jnp.floor(places)
    weight = (places - floors)[:, None, :]
    low_index = jnp.broadcast_to(floors.astype(jnp.int32)[:, None, :], filtered.shape)
    left_vals = jnp.take_along_axis(filtered, low_index, axis=2)
    right_vals = jnp.take_along_axis(filtered, low_index + 1, axis=2)
    return ((1.0 - weight) * left_vals + weight * right_vals).astype(jnp.bfloat16)

def reference(dual_field, forward, sinogram, first_weight, first_bias, middle_weight, middle_bias, last_weight, magnify, detector_shift, row_fraction, offsets, slab_order):
    stacked = jnp.stack([dual_field, forward, sinogram], axis=0).transpose(2, 0, 1, 3)

    def row_update(row_data):
        first_act = jax.nn.silu(conv_taps(wrap_angles(row_data), first_weight) + first_bias[:, None, None]).astype(jnp.bfloat16)
        second_act = jax.nn.silu(conv_taps(wrap_angles(first_act), middle_weight) + middle_bias[:, None, None]).astype(jnp.bfloat16)
        return conv_taps(wrap_angles(second_act), last_weight)[0]
    update = lax.map(row_update, stacked)
    new_dual = (dual_field.astype(jnp.float32) + update.transpose(1, 0, 2)).astype(jnp.bfloat16)
    filtered = jnp.dot(new_dual.reshape(ANGLES * R, U), ramp_block(0, U, U), preferred_element_type=jnp.float32).reshape(ANGLES, R, U)
    projected = interpolate(filtered, magnify, detector_shift)

    def per_block(running, block_id):
        block_rows = lax.dynamic_slice_in_dim(projected, block_id * ANG_DEV, ANG_DEV, 0)
        fraction = lax.dynamic_slice_in_dim(row_fraction, block_id * ANG_DEV, ANG_DEV, 0).astype(jnp.float32)[:, None, None]
        starts = offsets[block_id][slab_order]
        first_rows = (starts[:, None] + jnp.arange(SLAB_Z, dtype=jnp.int32)[None, :]).reshape(-1)
        lower_rows = jnp.take(block_rows, first_rows, axis=1).astype(jnp.float32)
        upper_rows = jnp.take(block_rows, first_rows + 1, axis=1).astype(jnp.float32)
        return (running + lax.optimization_barrier(jnp.sum((1.0 - fraction) * lower_rows + fraction * upper_rows, axis=0)), None)
    summed, _ = lax.scan(per_block, jnp.zeros((SLABS * SLAB_Z, U), jnp.float32), jnp.arange(BLOCKS, dtype=jnp.int32))
    volume = summed / math.sqrt(ANGLES)
    return (new_dual, volume)
```

```python
import math

import jax
import jax.numpy as jnp
import numpy as np
from jax import lax
from jax.experimental import pallas as pl
from jax.experimental.pallas import tpu as pltpu
from jax.sharding import PartitionSpec as P

U = 2048
CH = 32
ANG_DEV = 4
ROWS_DEV = 2
HALO = 3
FIELDS = 3
SLAB_Z = 4
SLABS_DEV = 4
BLOCKS = 16
ROW_DEVS = 16
LANES = 128
TILES = U // LANES
BLK = 256
NBLK = U // BLK
SPAN = ANG_DEV + 2 * HALO
ROWS1 = ROWS_DEV * (SPAN - 2) * CH
HALF1 = (SPAN - 2) * CH
HALF2 = (SPAN - 4) * CH
OUT8 = ANG_DEV * ROWS_DEV
CENTRE = (U - 1) / 2.0
MIB = 1024 * 1024
MAG_LOW, MAG_HIGH, SHIFT_MAX = 0.85, 0.95, 8.0


def ramp_tiles():
    row_ids = np.arange(BLK, dtype=np.int32)[None, :, None]
    col_ids = np.arange(BLK, dtype=np.int32)[None, None, :]
    gaps = np.arange(-(NBLK - 1), NBLK, dtype=np.int32)[:, None, None] * BLK
    diff = row_ids - (col_ids + gaps)
    odd = np.abs(diff) % 2 == 1
    distance = np.where(odd, diff, 1).astype(np.float32)
    falloff = np.float32(-1.0) / (np.float32(math.pi * math.pi) * distance * distance)
    tiles = np.where(diff == 0, np.float32(0.25), np.where(odd, falloff, np.float32(0.0)))
    return jnp.asarray(tiles.astype(np.float32)).astype(jnp.bfloat16)


def shifted(value, step):
    lane = lax.broadcasted_iota(jnp.int32, value.shape, 1)
    if step < 0:
        return jnp.where(lane == 0, 0.0, pltpu.roll(value, 1, 1))
    return jnp.where(lane == U - 1, 0.0, pltpu.roll(value, U - 1, 1))


def silu(value):
    half = 0.5 * value
    return half + half * jnp.tanh(half)


def source_tiles(tile):
    ends = []
    for column in (tile * LANES, tile * LANES + LANES - 1):
        for mag in (MAG_LOW, MAG_HIGH):
            for shift in (-SHIFT_MAX, SHIFT_MAX):
                ends.append((column - CENTRE) * mag + CENTRE + shift)
    low = int(math.floor(min(ends) - 0.5))
    high = int(math.floor(max(ends) + 0.5)) + 1
    return max(low, 0) // LANES, min(high, U - 1) // LANES


def pack_kernel(dual_hbm, forw_hbm, sino_hbm, out_ref, sems):
    loads = [
        pltpu.make_async_copy(field, out_ref.at[pl.ds(at * ANG_DEV, ANG_DEV)], sems.at[at])
        for at, field in enumerate((dual_hbm, forw_hbm, sino_hbm))
    ]
    for load in loads:
        load.start()
    for load in loads:
        load.wait()


def layout_kernel(
    first_ref, middle_ref, last_ref, bias1_ref, bias2_ref, order_ref, offs_ref,
    w1_ref, w2_ref, w3_ref, col1_ref, col2_ref, pick_ref,
    gather1, base2, base3,
):
    f32, bf16 = jnp.float32, jnp.bfloat16
    gather1[...] = jnp.zeros(gather1.shape, f32)
    for part in range(9):
        gather1[3 * part:3 * part + 3, 0:CH] = first_ref[part].astype(f32)
    key = lax.broadcasted_iota(jnp.int32, (32, 256), 0)
    lane = lax.broadcasted_iota(jnp.int32, (32, 256), 1)
    wanted = (key // 3 % 3) * 64 + (key % 3) * (2 * SPAN) + (key // 9) * 2
    spread = jnp.where((lane == wanted) & (key < 27), 1.0, 0.0)
    base1 = lax.dot_general(
        gather1[...].astype(bf16), spread.astype(bf16), (((0,), (0,)), ((), ())), preferred_element_type=f32
    )[0:CH]
    for row in range(ROWS_DEV):
        for ang in range(SPAN - 2):
            shift = 2 * ang + row
            rolled = pltpu.roll(base1, shift, 1) if shift else base1
            start = (row * (SPAN - 2) + ang) * CH
            w1_ref[start:start + CH, :] = rolled.astype(bf16)
    base2[...] = jnp.zeros(base2.shape, f32)
    for ang_tap in range(3):
        for tap in range(3):
            block = middle_ref[3 * ang_tap + tap].astype(f32)
            base2[tap * CH:(tap + 1) * CH, ang_tap * CH:(ang_tap + 1) * CH] = block
    for tap in range(3):
        wide = base2[tap * CH:(tap + 1) * CH, :]
        for ang in range(SPAN - 4):
            rolled = pltpu.roll(wide, CH * ang, 1) if ang else wide
            start = tap * HALF2 + ang * CH
            w2_ref[start:start + CH, :] = rolled.astype(bf16)
    base3[...] = jnp.zeros(base3.shape, f32)
    for ang_tap in range(3):
        base3[0:3, ang_tap * CH:(ang_tap + 1) * CH] = last_ref[ang_tap].astype(f32)
    wide = base3[...]
    for ang in range(ANG_DEV):
        for row in range(ROWS_DEV):
            shift = CH * ang + HALF2 * row
            rolled = pltpu.roll(wide, shift, 1) if shift else wide
            for tap in range(3):
                at = tap * OUT8 + ang * ROWS_DEV + row
                w3_ref[at:at + 1, :] = rolled[tap:tap + 1, :]
    square = (CH, CH)
    eye = lax.broadcasted_iota(jnp.int32, square, 0) == lax.broadcasted_iota(jnp.int32, square, 1)
    for bias_ref, col_ref in ((bias1_ref, col1_ref), (bias2_ref, col2_ref)):
        column = jnp.sum(jnp.where(eye, jnp.broadcast_to(bias_ref[...], square), 0.0), axis=1, keepdims=True)
        col_ref[...] = jnp.broadcast_to(column, (CH, LANES))
    slabs = SLABS_DEV * ROW_DEVS
    chosen = jnp.broadcast_to(order_ref[...], (slabs, slabs)) == lax.broadcasted_iota(jnp.int32, (slabs, slabs), 0)
    chosen = jnp.where(chosen, 1.0, 0.0).astype(bf16)
    starts = jnp.dot(offs_ref[...].astype(f32).astype(bf16), chosen, preferred_element_type=f32)
    width = 3 * 4 * BLOCKS
    block_of = (lax.broadcasted_iota(jnp.int32, (BLOCKS, width), 1) % (4 * BLOCKS)) // 4
    widen = jnp.where(block_of == lax.broadcasted_iota(jnp.int32, (BLOCKS, width), 0), 1.0, 0.0).astype(bf16)
    starts = lax.dot_general(
        starts.astype(bf16), widen, (((0,), (0,)), ((), ())), preferred_element_type=f32
    )
    rows = slabs * SLAB_Z
    slot_of = lax.broadcasted_iota(jnp.int32, (rows, slabs), 0) // SLAB_Z
    tall = jnp.where(slot_of == lax.broadcasted_iota(jnp.int32, (rows, slabs), 1), 1.0, 0.0).astype(bf16)
    starts = jnp.dot(tall, starts.astype(bf16), preferred_element_type=f32)
    depth = lax.broadcasted_iota(jnp.int32, (rows, width), 0) % SLAB_Z
    kind = lax.broadcasted_iota(jnp.int32, (rows, width), 1) % 4
    offset = depth + kind // 2 - kind % 2 - ROWS_DEV * lax.axis_index("row")
    pick_ref[...] = jnp.where(starts + offset.astype(f32) == 0.0, 1.0, 0.0).astype(bf16)


def field_kernel(
    mag_hbm, move_hbm, frac_hbm, ramp_hbm, own_ref, even_ref, odd_ref,
    w1_ref, w2_ref, w3_ref, col1_ref, col2_ref,
    dual_hbm, send_ref,
    x32, xcat, act1, taps2, act2, ramp_ref, dual_ref, mag_ref, move_ref, frac_ref, sems,
):
    f32, bf16 = jnp.float32, jnp.bfloat16
    loads = [
        pltpu.make_async_copy(mag_hbm, mag_ref, sems.at[0]),
        pltpu.make_async_copy(move_hbm, move_ref, sems.at[1]),
        pltpu.make_async_copy(frac_hbm, frac_ref, sems.at[2]),
        pltpu.make_async_copy(ramp_hbm, ramp_ref, sems.at[3]),
    ]
    for load in loads:
        load.start()
    x32[3 * 2 * SPAN:64, :] = jnp.zeros((64 - 3 * 2 * SPAN, U), f32)

    def lay(left_ref, right_ref):
        for field in range(FIELDS):
            base = field * 2 * SPAN
            for ang in range(HALO):
                x32[base + 2 * ang:base + 2 * ang + 2, :] = left_ref[field * ANG_DEV + 1 + ang].astype(f32)
                at = base + 2 * (HALO + ANG_DEV + ang)
                x32[at:at + 2, :] = right_ref[field * ANG_DEV + ang].astype(f32)

    for field in range(FIELDS):
        for ang in range(ANG_DEV):
            at = field * 2 * SPAN + 2 * (HALO + ang)
            x32[at:at + 2, :] = own_ref[field * ANG_DEV + ang].astype(f32)
    parity = lax.axis_index("ang") % 2

    @pl.when(parity == 0)
    def _():
        lay(odd_ref, even_ref)

    @pl.when(parity == 1)
    def _():
        lay(even_ref, odd_ref)

    stacked = x32[...]
    xcat[0:64, :] = shifted(stacked, -1).astype(bf16)
    xcat[64:128, :] = stacked.astype(bf16)
    xcat[128:192, :] = shifted(stacked, 1).astype(bf16)
    xcat[192:256, :] = jnp.zeros((64, U), bf16)

    bias1 = col1_ref[:, 0:1]

    def first_layer(step, carry):
        cols = pl.ds(pl.multiple_of(step * BLK, BLK), BLK)
        block = jnp.dot(w1_ref[...], xcat[:, cols], preferred_element_type=f32)
        for part in range(ROWS1 // CH):
            rows = slice(part * CH, (part + 1) * CH)
            act1[rows, cols] = silu(block[rows] + bias1).astype(bf16)
        return carry

    lax.fori_loop(0, NBLK, first_layer, 0)

    def second_dots(step, carry):
        cols = pl.ds(pl.multiple_of(step * BLK, BLK), BLK)
        for row in range(ROWS_DEV):
            taps2[row, :, cols] = jnp.dot(
                w2_ref[...], act1[row * HALF1:(row + 1) * HALF1, cols], preferred_element_type=f32
            )
        return carry

    lax.fori_loop(0, NBLK, second_dots, 0)

    bias2 = col2_ref[:, 0:1]

    def second_sum(step, carry):
        start = pl.multiple_of(step * CH, CH)
        for row in range(ROWS_DEV):
            before = shifted(taps2[row, pl.ds(start, CH), :], -1)
            here = taps2[row, pl.ds(HALF2 + start, CH), :]
            after = shifted(taps2[row, pl.ds(2 * HALF2 + start, CH), :], 1)
            total = before + here + after + bias2
            act2[pl.ds(row * HALF2 + start, CH), :] = silu(total).astype(bf16)
        return carry

    lax.fori_loop(0, HALF2 // CH, second_sum, 0)

    taps3 = jnp.dot(w3_ref[...].astype(bf16), act2[...], preferred_element_type=f32)
    update = shifted(taps3[0:8], -1) + taps3[8:16] + shifted(taps3[16:24], 1)
    own_dual = x32[2 * HALO:2 * HALO + OUT8, :]
    new_dual = (own_dual + update).astype(bf16)
    for ang in range(ANG_DEV):
        dual_ref[ang] = new_dual[2 * ang:2 * ang + 2, :]
    store = pltpu.make_async_copy(dual_ref, dual_hbm, sems.at[4])
    store.start()
    for load in loads:
        load.wait()
    dual32 = new_dual.astype(f32)
    blocks = jnp.concatenate([dual32[:, b * BLK:(b + 1) * BLK] for b in range(NBLK)], axis=0).astype(bf16)
    filtered = [None] * NBLK
    for gap in range(-(NBLK - 1), NBLK):
        part = jnp.dot(blocks, ramp_ref[gap + NBLK - 1], preferred_element_type=f32)
        for source in range(NBLK):
            target = source + gap
            if 0 <= target < NBLK:
                piece = part[source * OUT8:(source + 1) * OUT8]
                filtered[target] = piece if filtered[target] is None else filtered[target] + piece
    lanes = [filtered[t // 2][:, (t % 2) * LANES:(t % 2 + 1) * LANES] for t in range(TILES)]
    row_id = lax.broadcasted_iota(jnp.int32, (OUT8, LANES), 0)
    lane_id = lax.broadcasted_iota(jnp.int32, (OUT8, LANES), 1)
    ang_id = row_id // ROWS_DEV

    def per_angle(ref):
        value = jnp.full((OUT8, LANES), ref[0], f32)
        for ang in range(1, ANG_DEV):
            value = jnp.where(ang_id == ang, ref[ang], value)
        return value

    mag, move, frac = per_angle(mag_ref), per_angle(move_ref), per_angle(frac_ref)
    keep = 1.0 - frac
    for tile in range(TILES):
        column = (lane_id + tile * LANES).astype(f32)
        place = (column - CENTRE) * mag + CENTRE + move
        floor = jnp.floor(place)
        weight = place - floor
        low = floor.astype(jnp.int32)
        high = low + 1
        first, last = source_tiles(tile)
        left = jnp.zeros((OUT8, LANES), f32)
        right = jnp.zeros((OUT8, LANES), f32)
        for source in range(first, last + 1):
            got = jnp.take_along_axis(lanes[source], low & (LANES - 1), axis=1, mode="promise_in_bounds")
            left = jnp.where(low // LANES == source, got, left)
            got = jnp.take_along_axis(lanes[source], high & (LANES - 1), axis=1, mode="promise_in_bounds")
            right = jnp.where(high // LANES == source, got, right)
        projected = ((1.0 - weight) * left + weight * right).astype(bf16).astype(f32)
        lower = keep * projected
        upper = frac * projected
        lower = lower + pltpu.roll(lower, 4, 0)
        lower = lower + pltpu.roll(lower, 2, 0)
        upper = upper + pltpu.roll(upper, 4, 0)
        upper = upper + pltpu.roll(upper, 2, 0)
        packed = jnp.where(row_id < ROWS_DEV, lower, upper)
        send_ref[tile] = packed[0:4]
    store.wait()


def place_kernel(pick_ref, got_ref, out_ref):
    f32, bf16 = jnp.float32, jnp.bfloat16
    rows = got_ref[...]
    high = rows.astype(bf16)
    rest = rows - high.astype(f32)
    mid = rest.astype(bf16)
    low = (rest - mid.astype(f32)).astype(bf16)
    parts = jnp.concatenate([high, mid, low], axis=0)
    out_ref[...] = jnp.dot(pick_ref[...], parts, preferred_element_type=f32)


def in_hbm(value):
    return pltpu.with_memory_space_constraint(value, pltpu.HBM)


def per_device(
    dual_field, forward, sinogram, first_weight, first_bias, middle_weight, middle_bias, last_weight,
    magnify, detector_shift, row_fraction, offsets, slab_order,
):
    f32, bf16 = jnp.float32, jnp.bfloat16
    vmem = pl.BlockSpec(memory_space=pltpu.VMEM)
    hbm = pl.BlockSpec(memory_space=pltpu.HBM)
    own = pl.pallas_call(
        pack_kernel,
        out_shape=jax.ShapeDtypeStruct((FIELDS * ANG_DEV, ROWS_DEV, U), bf16),
        in_specs=[hbm] * 3,
        out_specs=vmem,
        scratch_shapes=[pltpu.SemaphoreType.DMA((3,))],
        compiler_params=pltpu.CompilerParams(vmem_limit_bytes=2 * MIB),
        name="pack_kernel",
    )(*map(in_hbm, (dual_field, forward, sinogram)))
    count = lax.axis_size("ang")
    even = lax.ppermute(own, "ang", [(i, i ^ 1) for i in range(count)])
    odd = lax.ppermute(own, "ang", [(i, (i + 1 if i % 2 else i - 1) % count) for i in range(count)])
    width = 3 * 4 * BLOCKS
    w1, w2, w3, col1, col2, pick = pl.pallas_call(
        layout_kernel,
        out_shape=(
            jax.ShapeDtypeStruct((ROWS1, 256), bf16),
            jax.ShapeDtypeStruct((3 * HALF2, HALF1), bf16),
            jax.ShapeDtypeStruct((24, 2 * HALF2), f32),
            jax.ShapeDtypeStruct((CH, LANES), f32),
            jax.ShapeDtypeStruct((CH, LANES), f32),
            jax.ShapeDtypeStruct((SLABS_DEV * ROW_DEVS * SLAB_Z, width), bf16),
        ),
        out_specs=(vmem,) * 6,
        scratch_shapes=[
            pltpu.VMEM((32, LANES), f32),
            pltpu.VMEM((3 * CH, HALF1), f32),
            pltpu.VMEM((8, 2 * HALF2), f32),
        ],
        compiler_params=pltpu.CompilerParams(vmem_limit_bytes=8 * MIB),
        name="layout_kernel",
    )(*map(in_hbm, (
        first_weight.transpose(0, 1, 3, 2).reshape(9, FIELDS, CH), middle_weight.reshape(9, CH, CH),
        last_weight.transpose(0, 2, 1, 3).reshape(3, 3, CH), first_bias[None], middle_bias[None],
        slab_order[None], offsets,
    )))
    new_dual, send = pl.pallas_call(
        field_kernel,
        out_shape=(
            jax.ShapeDtypeStruct((ANG_DEV, ROWS_DEV, U), bf16),
            jax.ShapeDtypeStruct((BLOCKS, 4, LANES), f32),
        ),
        in_specs=[hbm] * 4 + [vmem] * 8,
        out_specs=(hbm, vmem),
        scratch_shapes=[
            pltpu.VMEM((64, U), f32),
            pltpu.VMEM((256, U), bf16),
            pltpu.VMEM((ROWS1, U), bf16),
            pltpu.VMEM((ROWS_DEV, 3 * HALF2, U), f32),
            pltpu.VMEM((2 * HALF2, U), bf16),
            pltpu.VMEM((2 * NBLK - 1, BLK, BLK), bf16),
            pltpu.VMEM((ANG_DEV, ROWS_DEV, U), bf16),
            pltpu.SMEM((ANG_DEV,), f32),
            pltpu.SMEM((ANG_DEV,), f32),
            pltpu.SMEM((ANG_DEV,), f32),
            pltpu.SemaphoreType.DMA((5,)),
        ],
        compiler_params=pltpu.CompilerParams(vmem_limit_bytes=32 * MIB),
        name="field_kernel",
    )(*map(in_hbm, (magnify, detector_shift, row_fraction, ramp_tiles())), own, even, odd, w1, w2, w3, col1, col2)
    got = lax.all_to_all(send, "ang", 0, 0, tiled=True)
    placed = pl.pallas_call(
        place_kernel,
        out_shape=jax.ShapeDtypeStruct((SLABS_DEV * ROW_DEVS * SLAB_Z, LANES), f32),
        in_specs=[vmem, vmem],
        out_specs=vmem,
        compiler_params=pltpu.CompilerParams(vmem_limit_bytes=4 * MIB),
        name="place_kernel",
    )(pick, got.reshape(4 * BLOCKS, LANES))
    shares = lax.all_to_all(placed.reshape(ROW_DEVS, SLABS_DEV * SLAB_Z, LANES), "row", 0, 0, tiled=True)
    return new_dual, jnp.sum(shares, axis=0) * 0.125


def solution(mesh):
    field = P("ang", "row", None)
    return jax.shard_map(
        per_device,
        mesh=mesh,
        in_specs=(field, field, field) + (P(),) * 5 + (P("ang"),) * 3 + (P(), P()),
        out_specs=(field, P("row", "ang")),
        check_vma=False,
    )
```

```python
import math

import jax
import jax.numpy as jnp
import numpy as np
from jax import lax
from jax.experimental import pallas as pl
from jax.experimental.pallas import tpu as pltpu
from jax.sharding import PartitionSpec as P

U = 2048
CH = 32
ANG_DEV = 4
ROWS_DEV = 2
HALO = 3
FIELDS = 3
SLAB_Z = 4
SLABS_DEV = 4
BLOCKS = 16
ROW_DEVS = 16
LANES = 128
TILES = U // LANES
BLK = 256
NBLK = U // BLK
SPAN = ANG_DEV + 2 * HALO
ROWS1 = ROWS_DEV * (SPAN - 2) * CH
HALF1 = (SPAN - 2) * CH
HALF2 = (SPAN - 4) * CH
OUT8 = ANG_DEV * ROWS_DEV
CENTRE = (U - 1) / 2.0
MIB = 1024 * 1024
MAG_LOW, MAG_HIGH, SHIFT_MAX = 0.85, 0.95, 8.0


def ramp_tiles():
    row_ids = np.arange(BLK, dtype=np.int32)[None, :, None]
    col_ids = np.arange(BLK, dtype=np.int32)[None, None, :]
    gaps = np.arange(-(NBLK - 1), NBLK, dtype=np.int32)[:, None, None] * BLK
    diff = row_ids - (col_ids + gaps)
    odd = np.abs(diff) % 2 == 1
    distance = np.where(odd, diff, 1).astype(np.float32)
    falloff = np.float32(-1.0) / (np.float32(math.pi * math.pi) * distance * distance)
    tiles = np.where(diff == 0, np.float32(0.25), np.where(odd, falloff, np.float32(0.0)))
    return jnp.asarray(tiles.astype(np.float32)).astype(jnp.bfloat16)


def shifted(value, step):
    lane = lax.broadcasted_iota(jnp.int32, value.shape, 1)
    if step < 0:
        return jnp.where(lane == 0, 0.0, pltpu.roll(value, 1, 1))
    return jnp.where(lane == U - 1, 0.0, pltpu.roll(value, U - 1, 1))


def silu(value):
    half = 0.5 * value
    return half + half * jnp.tanh(half)


def source_tiles(tile):
    ends = []
    for column in (tile * LANES, tile * LANES + LANES - 1):
        for mag in (MAG_LOW, MAG_HIGH):
            for shift in (-SHIFT_MAX, SHIFT_MAX):
                ends.append((column - CENTRE) * mag + CENTRE + shift)
    low = int(math.floor(min(ends) - 0.5))
    high = int(math.floor(max(ends) + 0.5)) + 1
    return max(low, 0) // LANES, min(high, U - 1) // LANES


def pack_kernel(dual_hbm, forw_hbm, sino_hbm, out_ref, sems):
    loads = [
        pltpu.make_async_copy(field, out_ref.at[pl.ds(at * ANG_DEV, ANG_DEV)], sems.at[at])
        for at, field in enumerate((dual_hbm, forw_hbm, sino_hbm))
    ]
    for load in loads:
        load.start()
    for load in loads:
        load.wait()


def layout_kernel(
    first_ref, middle_ref, last_ref, bias1_ref, bias2_ref, order_ref, offs_ref,
    w1_ref, w2_ref, w3_ref, col1_ref, col2_ref, pick_ref,
    gather1, base2, base3,
):
    f32, bf16 = jnp.float32, jnp.bfloat16
    gather1[...] = jnp.zeros(gather1.shape, f32)
    for part in range(9):
        gather1[3 * part:3 * part + 3, 0:CH] = first_ref[part].astype(f32)
    key = lax.broadcasted_iota(jnp.int32, (32, 256), 0)
    lane = lax.broadcasted_iota(jnp.int32, (32, 256), 1)
    wanted = (key // 3 % 3) * 64 + (key % 3) * (2 * SPAN) + (key // 9) * 2
    spread = jnp.where((lane == wanted) & (key < 27), 1.0, 0.0)
    base1 = lax.dot_general(
        gather1[...].astype(bf16), spread.astype(bf16), (((0,), (0,)), ((), ())), preferred_element_type=f32
    )[0:CH]
    for row in range(ROWS_DEV):
        for ang in range(SPAN - 2):
            shift = 2 * ang + row
            rolled = pltpu.roll(base1, shift, 1) if shift else base1
            start = (row * (SPAN - 2) + ang) * CH
            w1_ref[start:start + CH, :] = rolled.astype(bf16)
    base2[...] = jnp.zeros(base2.shape, f32)
    for ang_tap in range(3):
        for tap in range(3):
            block = middle_ref[3 * ang_tap + tap].astype(f32)
            base2[tap * CH:(tap + 1) * CH, ang_tap * CH:(ang_tap + 1) * CH] = block
    for tap in range(3):
        wide = base2[tap * CH:(tap + 1) * CH, :]
        for ang in range(SPAN - 4):
            rolled = pltpu.roll(wide, CH * ang, 1) if ang else wide
            w2_ref[ang * CH:(ang + 1) * CH, tap * HALF1:(tap + 1) * HALF1] = rolled.astype(bf16)
    base3[...] = jnp.zeros(base3.shape, f32)
    for ang_tap in range(3):
        base3[0:3, ang_tap * CH:(ang_tap + 1) * CH] = last_ref[ang_tap].astype(f32)
    wide = base3[...]
    for ang in range(ANG_DEV):
        for row in range(ROWS_DEV):
            shift = CH * ang + HALF2 * row
            rolled = pltpu.roll(wide, shift, 1) if shift else wide
            for tap in range(3):
                at = tap * OUT8 + ang * ROWS_DEV + row
                w3_ref[at:at + 1, :] = rolled[tap:tap + 1, :]
    square = (CH, CH)
    eye = lax.broadcasted_iota(jnp.int32, square, 0) == lax.broadcasted_iota(jnp.int32, square, 1)
    for bias_ref, col_ref in ((bias1_ref, col1_ref), (bias2_ref, col2_ref)):
        column = jnp.sum(jnp.where(eye, jnp.broadcast_to(bias_ref[...], square), 0.0), axis=1, keepdims=True)
        col_ref[...] = jnp.broadcast_to(column, (CH, LANES))
    slabs = SLABS_DEV * ROW_DEVS
    chosen = jnp.broadcast_to(order_ref[...], (slabs, slabs)) == lax.broadcasted_iota(jnp.int32, (slabs, slabs), 0)
    chosen = jnp.where(chosen, 1.0, 0.0).astype(bf16)
    starts = jnp.dot(offs_ref[...].astype(f32).astype(bf16), chosen, preferred_element_type=f32)
    width = 3 * 4 * BLOCKS
    block_of = (lax.broadcasted_iota(jnp.int32, (BLOCKS, width), 1) % (4 * BLOCKS)) // 4
    widen = jnp.where(block_of == lax.broadcasted_iota(jnp.int32, (BLOCKS, width), 0), 1.0, 0.0).astype(bf16)
    starts = lax.dot_general(
        starts.astype(bf16), widen, (((0,), (0,)), ((), ())), preferred_element_type=f32
    )
    rows = slabs * SLAB_Z
    slot_of = lax.broadcasted_iota(jnp.int32, (rows, slabs), 0) // SLAB_Z
    tall = jnp.where(slot_of == lax.broadcasted_iota(jnp.int32, (rows, slabs), 1), 1.0, 0.0).astype(bf16)
    starts = jnp.dot(tall, starts.astype(bf16), preferred_element_type=f32)
    depth = lax.broadcasted_iota(jnp.int32, (rows, width), 0) % SLAB_Z
    kind = lax.broadcasted_iota(jnp.int32, (rows, width), 1) % 4
    offset = depth + kind // 2 - kind % 2 - ROWS_DEV * lax.axis_index("row")
    pick_ref[...] = jnp.where(starts + offset.astype(f32) == 0.0, 1.0, 0.0).astype(bf16)


def field_kernel(
    mag_hbm, move_hbm, frac_hbm, ramp_hbm, own_ref, even_ref, odd_ref,
    w1_ref, w2_ref, w3_ref, col1_ref, col2_ref,
    dual_hbm, send_ref,
    x32, xcat, act1, act2, ramp_ref, dual_ref, mag_ref, move_ref, frac_ref, sems,
):
    f32, bf16 = jnp.float32, jnp.bfloat16
    loads = [
        pltpu.make_async_copy(mag_hbm, mag_ref, sems.at[0]),
        pltpu.make_async_copy(move_hbm, move_ref, sems.at[1]),
        pltpu.make_async_copy(frac_hbm, frac_ref, sems.at[2]),
        pltpu.make_async_copy(ramp_hbm, ramp_ref, sems.at[3]),
    ]
    for load in loads:
        load.start()
    x32[3 * 2 * SPAN:64, :] = jnp.zeros((64 - 3 * 2 * SPAN, U), f32)

    def lay(left_ref, right_ref):
        for field in range(FIELDS):
            base = field * 2 * SPAN
            for ang in range(HALO):
                x32[base + 2 * ang:base + 2 * ang + 2, :] = left_ref[field * ANG_DEV + 1 + ang].astype(f32)
                at = base + 2 * (HALO + ANG_DEV + ang)
                x32[at:at + 2, :] = right_ref[field * ANG_DEV + ang].astype(f32)

    for field in range(FIELDS):
        for ang in range(ANG_DEV):
            at = field * 2 * SPAN + 2 * (HALO + ang)
            x32[at:at + 2, :] = own_ref[field * ANG_DEV + ang].astype(f32)
    parity = lax.axis_index("ang") % 2

    @pl.when(parity == 0)
    def _():
        lay(odd_ref, even_ref)

    @pl.when(parity == 1)
    def _():
        lay(even_ref, odd_ref)

    stacked = x32[...]
    xcat[0:64, :] = shifted(stacked, -1).astype(bf16)
    xcat[64:128, :] = stacked.astype(bf16)
    xcat[128:192, :] = shifted(stacked, 1).astype(bf16)
    xcat[192:256, :] = jnp.zeros((64, U), bf16)

    bias1 = col1_ref[:, 0:1]
    bias2 = col2_ref[:, 0:1]
    edge = lax.broadcasted_iota(jnp.int32, (HALF1, LANES), 1)
    for row in range(ROWS_DEV):
        for step in range(NBLK):
            cols = slice(step * BLK, (step + 1) * BLK)
            block = jnp.dot(w1_ref[row * HALF1:(row + 1) * HALF1, :], xcat[:, cols], preferred_element_type=f32)
            for part in range(HALF1 // CH):
                rows = slice(part * CH, (part + 1) * CH)
                act1[row, HALF1 + part * CH:HALF1 + (part + 1) * CH, cols] = silu(block[rows] + bias1).astype(bf16)
        here = act1[row, HALF1:2 * HALF1, :]
        before = pltpu.roll(here, 1, 1)
        after = pltpu.roll(here, U - 1, 1)
        act1[row, 0:HALF1, LANES:] = before[:, LANES:]
        act1[row, 0:HALF1, 0:LANES] = jnp.where(edge == 0, 0.0, before[:, 0:LANES].astype(f32)).astype(bf16)
        act1[row, 2 * HALF1:, 0:U - LANES] = after[:, 0:U - LANES]
        last = after[:, U - LANES:].astype(f32)
        act1[row, 2 * HALF1:, U - LANES:] = jnp.where(edge == LANES - 1, 0.0, last).astype(bf16)
    for row in range(ROWS_DEV):
        for step in range(NBLK):
            cols = slice(step * BLK, (step + 1) * BLK)
            block = jnp.dot(w2_ref[...], act1[row, :, cols], preferred_element_type=f32)
            for part in range(HALF2 // CH):
                rows = slice(part * CH, (part + 1) * CH)
                act2[row * HALF2 + part * CH:row * HALF2 + (part + 1) * CH, cols] = (
                    silu(block[rows] + bias2).astype(bf16)
                )
    taps3 = jnp.dot(w3_ref[...].astype(bf16), act2[...], preferred_element_type=f32)
    update = shifted(taps3[0:8], -1) + taps3[8:16] + shifted(taps3[16:24], 1)
    own_dual = x32[2 * HALO:2 * HALO + OUT8, :]
    new_dual = (own_dual + update).astype(bf16)
    for ang in range(ANG_DEV):
        dual_ref[ang] = new_dual[2 * ang:2 * ang + 2, :]
    store = pltpu.make_async_copy(dual_ref, dual_hbm, sems.at[4])
    store.start()
    for load in loads:
        load.wait()
    dual32 = new_dual.astype(f32)
    blocks = jnp.concatenate([dual32[:, b * BLK:(b + 1) * BLK] for b in range(NBLK)], axis=0).astype(bf16)
    filtered = [None] * NBLK
    for gap in range(-(NBLK - 1), NBLK):
        part = jnp.dot(blocks, ramp_ref[gap + NBLK - 1], preferred_element_type=f32)
        for source in range(NBLK):
            target = source + gap
            if 0 <= target < NBLK:
                piece = part[source * OUT8:(source + 1) * OUT8]
                filtered[target] = piece if filtered[target] is None else filtered[target] + piece
    lanes = [filtered[t // 2][:, (t % 2) * LANES:(t % 2 + 1) * LANES] for t in range(TILES)]
    row_id = lax.broadcasted_iota(jnp.int32, (OUT8, LANES), 0)
    lane_id = lax.broadcasted_iota(jnp.int32, (OUT8, LANES), 1)
    ang_id = row_id // ROWS_DEV

    def per_angle(ref):
        value = jnp.full((OUT8, LANES), ref[0], f32)
        for ang in range(1, ANG_DEV):
            value = jnp.where(ang_id == ang, ref[ang], value)
        return value

    mag, move, frac = per_angle(mag_ref), per_angle(move_ref), per_angle(frac_ref)
    keep = 1.0 - frac
    for tile in range(TILES):
        column = (lane_id + tile * LANES).astype(f32)
        place = (column - CENTRE) * mag + CENTRE + move
        floor = jnp.floor(place)
        weight = place - floor
        low = floor.astype(jnp.int32)
        high = low + 1
        first, last = source_tiles(tile)
        left = jnp.zeros((OUT8, LANES), f32)
        right = jnp.zeros((OUT8, LANES), f32)
        for source in range(first, last + 1):
            got = jnp.take_along_axis(lanes[source], low & (LANES - 1), axis=1, mode="promise_in_bounds")
            left = jnp.where(low // LANES == source, got, left)
            got = jnp.take_along_axis(lanes[source], high & (LANES - 1), axis=1, mode="promise_in_bounds")
            right = jnp.where(high // LANES == source, got, right)
        projected = ((1.0 - weight) * left + weight * right).astype(bf16).astype(f32)
        lower = keep * projected
        upper = frac * projected
        lower = lower + pltpu.roll(lower, 4, 0)
        lower = lower + pltpu.roll(lower, 2, 0)
        upper = upper + pltpu.roll(upper, 4, 0)
        upper = upper + pltpu.roll(upper, 2, 0)
        packed = jnp.where(row_id < ROWS_DEV, lower, upper)
        send_ref[tile] = packed[0:4]
    store.wait()


def place_kernel(pick_ref, got_ref, out_ref):
    f32, bf16 = jnp.float32, jnp.bfloat16
    rows = got_ref[...]
    high = rows.astype(bf16)
    rest = rows - high.astype(f32)
    mid = rest.astype(bf16)
    low = (rest - mid.astype(f32)).astype(bf16)
    parts = jnp.concatenate([high, mid, low], axis=0)
    out_ref[...] = jnp.dot(pick_ref[...], parts, preferred_element_type=f32)


def in_hbm(value):
    return pltpu.with_memory_space_constraint(value, pltpu.HBM)


def per_device(
    dual_field, forward, sinogram, first_weight, first_bias, middle_weight, middle_bias, last_weight,
    magnify, detector_shift, row_fraction, offsets, slab_order,
):
    f32, bf16 = jnp.float32, jnp.bfloat16
    vmem = pl.BlockSpec(memory_space=pltpu.VMEM)
    hbm = pl.BlockSpec(memory_space=pltpu.HBM)
    own = pl.pallas_call(
        pack_kernel,
        out_shape=jax.ShapeDtypeStruct((FIELDS * ANG_DEV, ROWS_DEV, U), bf16),
        in_specs=[hbm] * 3,
        out_specs=vmem,
        scratch_shapes=[pltpu.SemaphoreType.DMA((3,))],
        compiler_params=pltpu.CompilerParams(vmem_limit_bytes=2 * MIB),
        name="pack_kernel",
    )(*map(in_hbm, (dual_field, forward, sinogram)))
    count = lax.axis_size("ang")
    even = lax.ppermute(own, "ang", [(i, i ^ 1) for i in range(count)])
    odd = lax.ppermute(own, "ang", [(i, (i + 1 if i % 2 else i - 1) % count) for i in range(count)])
    width = 3 * 4 * BLOCKS
    w1, w2, w3, col1, col2, pick = pl.pallas_call(
        layout_kernel,
        out_shape=(
            jax.ShapeDtypeStruct((ROWS1, 256), bf16),
            jax.ShapeDtypeStruct((HALF2, 3 * HALF1), bf16),
            jax.ShapeDtypeStruct((24, 2 * HALF2), f32),
            jax.ShapeDtypeStruct((CH, LANES), f32),
            jax.ShapeDtypeStruct((CH, LANES), f32),
            jax.ShapeDtypeStruct((SLABS_DEV * ROW_DEVS * SLAB_Z, width), bf16),
        ),
        out_specs=(vmem,) * 6,
        scratch_shapes=[
            pltpu.VMEM((32, LANES), f32),
            pltpu.VMEM((3 * CH, HALF1), f32),
            pltpu.VMEM((8, 2 * HALF2), f32),
        ],
        compiler_params=pltpu.CompilerParams(vmem_limit_bytes=8 * MIB),
        name="layout_kernel",
    )(*map(in_hbm, (
        first_weight.transpose(0, 1, 3, 2).reshape(9, FIELDS, CH), middle_weight.reshape(9, CH, CH),
        last_weight.transpose(0, 2, 1, 3).reshape(3, 3, CH), first_bias[None], middle_bias[None],
        slab_order[None], offsets,
    )))
    new_dual, send = pl.pallas_call(
        field_kernel,
        out_shape=(
            jax.ShapeDtypeStruct((ANG_DEV, ROWS_DEV, U), bf16),
            jax.ShapeDtypeStruct((BLOCKS, 4, LANES), f32),
        ),
        in_specs=[hbm] * 4 + [vmem] * 8,
        out_specs=(hbm, vmem),
        scratch_shapes=[
            pltpu.VMEM((64, U), f32),
            pltpu.VMEM((256, U), bf16),
            pltpu.VMEM((ROWS_DEV, 3 * HALF1, U), bf16),
            pltpu.VMEM((2 * HALF2, U), bf16),
            pltpu.VMEM((2 * NBLK - 1, BLK, BLK), bf16),
            pltpu.VMEM((ANG_DEV, ROWS_DEV, U), bf16),
            pltpu.SMEM((ANG_DEV,), f32),
            pltpu.SMEM((ANG_DEV,), f32),
            pltpu.SMEM((ANG_DEV,), f32),
            pltpu.SemaphoreType.DMA((5,)),
        ],
        compiler_params=pltpu.CompilerParams(vmem_limit_bytes=32 * MIB),
        name="field_kernel",
    )(*map(in_hbm, (magnify, detector_shift, row_fraction, ramp_tiles())), own, even, odd, w1, w2, w3, col1, col2)
    got = lax.all_to_all(send, "ang", 0, 0, tiled=True)
    placed = pl.pallas_call(
        place_kernel,
        out_shape=jax.ShapeDtypeStruct((SLABS_DEV * ROW_DEVS * SLAB_Z, LANES), f32),
        in_specs=[vmem, vmem],
        out_specs=vmem,
        compiler_params=pltpu.CompilerParams(vmem_limit_bytes=4 * MIB),
        name="place_kernel",
    )(pick, got.reshape(4 * BLOCKS, LANES))
    shares = lax.all_to_all(placed.reshape(ROW_DEVS, SLABS_DEV * SLAB_Z, LANES), "row", 0, 0, tiled=True)
    return new_dual, jnp.sum(shares, axis=0) * 0.125


def solution(mesh):
    field = P("ang", "row", None)
    return jax.shard_map(
        per_device,
        mesh=mesh,
        in_specs=(field, field, field) + (P(),) * 5 + (P("ang"),) * 3 + (P(), P()),
        out_specs=(field, P("row", "ang")),
        check_vma=False,
    )
```

```python
import math

import jax
import jax.numpy as jnp
import numpy as np
from jax import lax
from jax.experimental import pallas as pl
from jax.experimental.pallas import tpu as pltpu
from jax.sharding import PartitionSpec as P

U = 2048
CH = 32
ANG_DEV = 4
ROWS_DEV = 2
HALO = 3
FIELDS = 3
SLAB_Z = 4
SLABS_DEV = 4
BLOCKS = 16
ROW_DEVS = 16
LANES = 128
TILES = U // LANES
BLK = 256
NBLK = U // BLK
SPAN = ANG_DEV + 2 * HALO
ROWS1 = ROWS_DEV * (SPAN - 2) * CH
HALF1 = (SPAN - 2) * CH
GROUP1 = 5 * CH
GROUP2 = 3 * CH
OUT8 = ANG_DEV * ROWS_DEV
CENTRE = (U - 1) / 2.0
MIB = 1024 * 1024
MAG_LOW, MAG_HIGH, SHIFT_MAX = 0.85, 0.95, 8.0


def ramp_tiles():
    row_ids = np.arange(BLK, dtype=np.int32)[None, :, None]
    col_ids = np.arange(BLK, dtype=np.int32)[None, None, :]
    gaps = np.arange(-(NBLK - 1), NBLK, dtype=np.int32)[:, None, None] * BLK
    diff = row_ids - (col_ids + gaps)
    odd = np.abs(diff) % 2 == 1
    distance = np.where(odd, diff, 1).astype(np.float32)
    falloff = np.float32(-1.0) / (np.float32(math.pi * math.pi) * distance * distance)
    tiles = np.where(diff == 0, np.float32(0.25), np.where(odd, falloff, np.float32(0.0)))
    return jnp.asarray(tiles.astype(np.float32)).astype(jnp.bfloat16)


def shifted(value, step):
    lane = lax.broadcasted_iota(jnp.int32, value.shape, 1)
    if step < 0:
        return jnp.where(lane == 0, 0.0, pltpu.roll(value, 1, 1))
    return jnp.where(lane == U - 1, 0.0, pltpu.roll(value, U - 1, 1))


def silu(value):
    half = 0.5 * value
    return half + half * jnp.tanh(half)


def source_tiles(tile):
    ends = []
    for column in (tile * LANES, tile * LANES + LANES - 1):
        for mag in (MAG_LOW, MAG_HIGH):
            for shift in (-SHIFT_MAX, SHIFT_MAX):
                ends.append((column - CENTRE) * mag + CENTRE + shift)
    low = int(math.floor(min(ends) - 0.5))
    high = int(math.floor(max(ends) + 0.5)) + 1
    return max(low, 0) // LANES, min(high, U - 1) // LANES


def parity():
    return lax.axis_index("ang") % 2


def turned(index, last):
    return index + parity() * (last - 2 * index)


def pack_kernel(dual_hbm, forw_hbm, sino_hbm, own_ref, far_ref, sems):
    loads = []
    for at, field in enumerate((dual_hbm, forw_hbm, sino_hbm)):
        side = field.at[pl.ds(parity(), HALO)]
        loads.append(pltpu.make_async_copy(side, far_ref.at[pl.ds(at * HALO, HALO)], sems.at[at]))
        loads.append(pltpu.make_async_copy(field, own_ref.at[pl.ds(at * ANG_DEV, ANG_DEV)], sems.at[3 + at]))
    for load in loads:
        load.start()
    for load in loads:
        load.wait()


def layout_kernel(
    first_ref, middle_ref, last_ref, bias1_ref, bias2_ref, order_ref, offs_ref,
    w1_ref, w2_ref, w3_ref, col1_ref, col2_ref, pick_ref,
    gather1, base2,
):
    f32, bf16 = jnp.float32, jnp.bfloat16
    gather1[...] = jnp.zeros(gather1.shape, f32)
    for ang_tap in range(3):
        for tap in range(3):
            part = 3 * ang_tap + tap
            gather1[3 * part:3 * part + 3, 0:CH] = first_ref[3 * turned(ang_tap, 2) + tap].astype(f32)
    key = lax.broadcasted_iota(jnp.int32, (32, 256), 0)
    lane = lax.broadcasted_iota(jnp.int32, (32, 256), 1)
    wanted = (key // 3 % 3) * 64 + (key % 3) * (2 * SPAN) + (key // 9) * 2
    spread = jnp.where((lane == wanted) & (key < 27), 1.0, 0.0)
    base1 = lax.dot_general(
        gather1[...].astype(bf16), spread.astype(bf16), (((0,), (0,)), ((), ())), preferred_element_type=f32
    )[0:CH]
    for row in range(ROWS_DEV):
        for ang in range(SPAN - 2):
            shift = 2 * ang + row
            rolled = pltpu.roll(base1, shift, 1) if shift else base1
            start = (row * (SPAN - 2) + ang) * CH
            w1_ref[start:start + CH, :] = rolled.astype(bf16)
    base2[...] = jnp.zeros(base2.shape, f32)
    for ang_tap in range(3):
        for tap in range(3):
            block = middle_ref[3 * turned(ang_tap, 2) + tap].astype(f32)
            for ang in range(3):
                start = tap * GROUP1 + (ang + ang_tap) * CH
                base2[ang * CH:(ang + 1) * CH, start:start + CH] = block
    w2_ref[...] = base2[...].astype(bf16)
    w3_ref[...] = jnp.zeros(w3_ref.shape, f32)
    for ang_tap in range(3):
        block = last_ref[turned(ang_tap, 2)].astype(f32)
        for ang in range(ANG_DEV):
            source = ang + ang_tap
            for row in range(ROWS_DEV):
                start = row * GROUP2 + source % 3 * CH
                for tap in range(3):
                    at = tap * OUT8 + ang * ROWS_DEV + row
                    w3_ref[source // 3, at:at + 1, start:start + CH] = block[tap:tap + 1, :]
    square = (CH, CH)
    eye = lax.broadcasted_iota(jnp.int32, square, 0) == lax.broadcasted_iota(jnp.int32, square, 1)
    for bias_ref, col_ref in ((bias1_ref, col1_ref), (bias2_ref, col2_ref)):
        column = jnp.sum(jnp.where(eye, jnp.broadcast_to(bias_ref[...], square), 0.0), axis=1, keepdims=True)
        col_ref[...] = jnp.broadcast_to(column, (CH, LANES))
    slabs = SLABS_DEV * ROW_DEVS
    chosen = jnp.broadcast_to(order_ref[...], (slabs, slabs)) == lax.broadcasted_iota(jnp.int32, (slabs, slabs), 0)
    chosen = jnp.where(chosen, 1.0, 0.0).astype(bf16)
    starts = jnp.dot(offs_ref[...].astype(f32).astype(bf16), chosen, preferred_element_type=f32)
    width = 3 * 4 * BLOCKS
    block_of = (lax.broadcasted_iota(jnp.int32, (BLOCKS, width), 1) % (4 * BLOCKS)) // 4
    widen = jnp.where(block_of == lax.broadcasted_iota(jnp.int32, (BLOCKS, width), 0), 1.0, 0.0).astype(bf16)
    starts = lax.dot_general(
        starts.astype(bf16), widen, (((0,), (0,)), ((), ())), preferred_element_type=f32
    )
    rows = slabs * SLAB_Z
    slot_of = lax.broadcasted_iota(jnp.int32, (rows, slabs), 0) // SLAB_Z
    tall = jnp.where(slot_of == lax.broadcasted_iota(jnp.int32, (rows, slabs), 1), 1.0, 0.0).astype(bf16)
    starts = jnp.dot(tall, starts.astype(bf16), preferred_element_type=f32)
    depth = lax.broadcasted_iota(jnp.int32, (rows, width), 0) % SLAB_Z
    kind = lax.broadcasted_iota(jnp.int32, (rows, width), 1) % 4
    offset = depth + kind // 2 - kind % 2 - ROWS_DEV * lax.axis_index("row")
    pick_ref[...] = jnp.where(starts + offset.astype(f32) == 0.0, 1.0, 0.0).astype(bf16)


def lay_inputs(x32, xcat, own_ref, side_ref, side, sent):
    f32, bf16 = jnp.float32, jnp.bfloat16
    x32[...] = jnp.zeros(x32.shape, f32)
    for field in range(FIELDS):
        base = field * 2 * SPAN
        for ang in range(ANG_DEV):
            at = base + 2 * (HALO + ang)
            x32[at:at + 2, :] = own_ref[field * ANG_DEV + turned(ang, ANG_DEV - 1)].astype(f32)
        for ang in range(HALO):
            at = base + 2 * (side + ang)
            x32[at:at + 2, :] = side_ref[field * sent + turned(ang, sent - 1)].astype(f32)
    stacked = x32[...]
    xcat[0:64, :] = shifted(stacked, -1).astype(bf16)
    xcat[64:128, :] = stacked.astype(bf16)
    xcat[128:192, :] = shifted(stacked, 1).astype(bf16)
    xcat[192:256, :] = jnp.zeros((64, U), bf16)


def first_layer(xcat, w1_ref, bias1, act1, row, first, count):
    f32, bf16 = jnp.float32, jnp.bfloat16
    start, size = row * HALF1 + first * CH, count * CH
    lane = lax.broadcasted_iota(jnp.int32, (size, LANES), 1)
    nothing = jnp.zeros((size, LANES), bf16)
    before_edge, after_rest = nothing, None
    for step in range(NBLK):
        cols = slice(step * BLK, (step + 1) * BLK)
        block = jnp.dot(w1_ref[start:start + size, :], xcat[:, cols], preferred_element_type=f32)
        act = jnp.concatenate(
            [silu(block[part * CH:(part + 1) * CH] + bias1) for part in range(count)], axis=0
        ).astype(bf16)
        act1[row, GROUP1:GROUP1 + size, cols] = act
        before = pltpu.roll(act, 1, 1)
        act1[row, 0:size, step * BLK:step * BLK + LANES] = jnp.where(lane == 0, before_edge, before[:, 0:LANES])
        act1[row, 0:size, step * BLK + LANES:(step + 1) * BLK] = before[:, LANES:]
        before_edge = before[:, 0:LANES]
        after = pltpu.roll(act, BLK - 1, 1)
        act1[row, 2 * GROUP1:2 * GROUP1 + size, step * BLK:step * BLK + LANES] = after[:, 0:LANES]
        if step:
            act1[row, 2 * GROUP1:2 * GROUP1 + size, step * BLK - LANES:step * BLK] = jnp.where(
                lane == LANES - 1, after[:, LANES:], after_rest
            )
        after_rest = after[:, LANES:]
    act1[row, 2 * GROUP1:2 * GROUP1 + size, U - LANES:] = jnp.where(lane == LANES - 1, nothing, after_rest)


def first_layer_whole(xcat, w1_ref, bias1, act1, row, first, count):
    f32, bf16 = jnp.float32, jnp.bfloat16
    start = row * HALF1 + first * CH
    for step in range(NBLK):
        cols = slice(step * BLK, (step + 1) * BLK)
        block = jnp.dot(w1_ref[start:start + count * CH, :], xcat[:, cols], preferred_element_type=f32)
        for part in range(count):
            rows = slice(GROUP1 + part * CH, GROUP1 + (part + 1) * CH)
            act1[row, rows, cols] = silu(block[part * CH:(part + 1) * CH] + bias1).astype(bf16)
    edge = lax.broadcasted_iota(jnp.int32, (CH, LANES), 1)
    for part in range(count):
        low, middle, high = (slice(tap * GROUP1 + part * CH, tap * GROUP1 + (part + 1) * CH) for tap in range(3))
        here = act1[row, middle, :]
        before = pltpu.roll(here, 1, 1)
        after = pltpu.roll(here, U - 1, 1)
        act1[row, low, LANES:] = before[:, LANES:]
        act1[row, low, 0:LANES] = jnp.where(edge == 0, 0.0, before[:, 0:LANES].astype(f32)).astype(bf16)
        act1[row, high, 0:U - LANES] = after[:, 0:U - LANES]
        last = after[:, U - LANES:].astype(f32)
        act1[row, high, U - LANES:] = jnp.where(edge == LANES - 1, 0.0, last).astype(bf16)


def second_layer(w2_ref, bias2, act1, act2):
    f32, bf16 = jnp.float32, jnp.bfloat16
    for row in range(ROWS_DEV):
        for step in range(NBLK):
            cols = slice(step * BLK, (step + 1) * BLK)
            block = jnp.dot(w2_ref[...], act1[row, :, cols], preferred_element_type=f32)
            for part in range(3):
                rows = slice(row * GROUP2 + part * CH, row * GROUP2 + (part + 1) * CH)
                act2[rows, cols] = silu(block[part * CH:(part + 1) * CH] + bias2).astype(bf16)


def near_kernel(
    ramp_hbm, own_ref, near_ref, w1_ref, w2_ref, w3_ref, col1_ref, col2_ref,
    shared_ref, taps_ref, ramp_ref,
    x32, xcat, act1, act2, sem,
):
    load = pltpu.make_async_copy(ramp_hbm, ramp_ref, sem)
    load.start()
    bias1, bias2 = col1_ref[:, 0:1], col2_ref[:, 0:1]
    lay_inputs(x32, xcat, own_ref, near_ref, HALO + ANG_DEV, ANG_DEV)
    for row in range(ROWS_DEV):
        first_layer_whole(xcat, w1_ref, bias1, act1, row, 3, 5)
        for tap in range(3):
            shared_ref[row, tap] = act1[row, tap * GROUP1:tap * GROUP1 + 2 * CH, :]
    second_layer(w2_ref, bias2, act1, act2)
    taps_ref[...] = jnp.dot(w3_ref[1].astype(jnp.bfloat16), act2[...], preferred_element_type=jnp.float32)
    load.wait()


def far_kernel(
    mag_hbm, move_hbm, frac_hbm, own_ref, far_ref, shared_ref, taps_ref, ramp_ref,
    w1_ref, w2_ref, w3_ref, col1_ref, col2_ref,
    dual_hbm, send_ref,
    x32, xcat, act1, act2, dual_ref, mag_ref, move_ref, frac_ref, sems,
):
    f32, bf16 = jnp.float32, jnp.bfloat16
    loads = [
        pltpu.make_async_copy(mag_hbm, mag_ref, sems.at[0]),
        pltpu.make_async_copy(move_hbm, move_ref, sems.at[1]),
        pltpu.make_async_copy(frac_hbm, frac_ref, sems.at[2]),
    ]
    for load in loads:
        load.start()
    bias1, bias2 = col1_ref[:, 0:1], col2_ref[:, 0:1]
    lay_inputs(x32, xcat, own_ref, far_ref, 0, HALO)
    for row in range(ROWS_DEV):
        first_layer(xcat, w1_ref, bias1, act1, row, 0, 3)
        for tap in range(3):
            act1[row, tap * GROUP1 + 3 * CH:(tap + 1) * GROUP1, :] = shared_ref[row, tap]
    second_layer(w2_ref, bias2, act1, act2)
    taps3 = taps_ref[...] + jnp.dot(w3_ref[0].astype(bf16), act2[...], preferred_element_type=f32)
    update = shifted(taps3[0:8], -1) + taps3[8:16] + shifted(taps3[16:24], 1)
    own_dual = x32[2 * HALO:2 * HALO + OUT8, :]
    new_dual = (own_dual + update).astype(bf16)
    for ang in range(ANG_DEV):
        dual_ref[turned(ang, ANG_DEV - 1)] = new_dual[2 * ang:2 * ang + 2, :]
    store = pltpu.make_async_copy(dual_ref, dual_hbm, sems.at[3])
    store.start()
    for load in loads:
        load.wait()
    dual32 = new_dual.astype(f32)
    blocks = jnp.concatenate([dual32[:, b * BLK:(b + 1) * BLK] for b in range(NBLK)], axis=0).astype(bf16)
    filtered = [None] * NBLK
    for gap in range(-(NBLK - 1), NBLK):
        part = jnp.dot(blocks, ramp_ref[gap + NBLK - 1], preferred_element_type=f32)
        for source in range(NBLK):
            target = source + gap
            if 0 <= target < NBLK:
                piece = part[source * OUT8:(source + 1) * OUT8]
                filtered[target] = piece if filtered[target] is None else filtered[target] + piece
    lanes = [filtered[t // 2][:, (t % 2) * LANES:(t % 2 + 1) * LANES] for t in range(TILES)]
    row_id = lax.broadcasted_iota(jnp.int32, (OUT8, LANES), 0)
    lane_id = lax.broadcasted_iota(jnp.int32, (OUT8, LANES), 1)
    ang_id = row_id // ROWS_DEV

    def per_angle(ref):
        value = jnp.full((OUT8, LANES), ref[turned(0, ANG_DEV - 1)], f32)
        for ang in range(1, ANG_DEV):
            value = jnp.where(ang_id == ang, ref[turned(ang, ANG_DEV - 1)], value)
        return value

    mag, move, frac = per_angle(mag_ref), per_angle(move_ref), per_angle(frac_ref)
    keep = 1.0 - frac
    for tile in range(TILES):
        column = (lane_id + tile * LANES).astype(f32)
        place = (column - CENTRE) * mag + CENTRE + move
        floor = jnp.floor(place)
        weight = place - floor
        low = floor.astype(jnp.int32)
        high = low + 1
        first, last = source_tiles(tile)
        left = jnp.zeros((OUT8, LANES), f32)
        right = jnp.zeros((OUT8, LANES), f32)
        for source in range(first, last + 1):
            got = jnp.take_along_axis(lanes[source], low & (LANES - 1), axis=1, mode="promise_in_bounds")
            left = jnp.where(low // LANES == source, got, left)
            got = jnp.take_along_axis(lanes[source], high & (LANES - 1), axis=1, mode="promise_in_bounds")
            right = jnp.where(high // LANES == source, got, right)
        projected = ((1.0 - weight) * left + weight * right).astype(bf16).astype(f32)
        lower = keep * projected
        upper = frac * projected
        lower = lower + pltpu.roll(lower, 4, 0)
        lower = lower + pltpu.roll(lower, 2, 0)
        upper = upper + pltpu.roll(upper, 4, 0)
        upper = upper + pltpu.roll(upper, 2, 0)
        packed = jnp.where(row_id < ROWS_DEV, lower, upper)
        send_ref[tile] = packed[0:4]
    store.wait()


def place_kernel(pick_ref, got_ref, out_ref):
    f32, bf16 = jnp.float32, jnp.bfloat16
    rows = got_ref[...]
    high = rows.astype(bf16)
    rest = rows - high.astype(f32)
    mid = rest.astype(bf16)
    low = (rest - mid.astype(f32)).astype(bf16)
    parts = jnp.concatenate([high, mid, low], axis=0)
    out_ref[...] = jnp.dot(pick_ref[...], parts, preferred_element_type=f32)


def in_hbm(value):
    return pltpu.with_memory_space_constraint(value, pltpu.HBM)


def per_device(
    dual_field, forward, sinogram, first_weight, first_bias, middle_weight, middle_bias, last_weight,
    magnify, detector_shift, row_fraction, offsets, slab_order,
):
    f32, bf16 = jnp.float32, jnp.bfloat16
    vmem = pl.BlockSpec(memory_space=pltpu.VMEM)
    hbm = pl.BlockSpec(memory_space=pltpu.HBM)
    own, far = pl.pallas_call(
        pack_kernel,
        out_shape=(
            jax.ShapeDtypeStruct((FIELDS * ANG_DEV, ROWS_DEV, U), bf16),
            jax.ShapeDtypeStruct((FIELDS * HALO, ROWS_DEV, U), bf16),
        ),
        in_specs=[hbm] * 3,
        out_specs=(vmem,) * 2,
        scratch_shapes=[pltpu.SemaphoreType.DMA((6,))],
        compiler_params=pltpu.CompilerParams(vmem_limit_bytes=2 * MIB),
        name="pack_kernel",
    )(*map(in_hbm, (dual_field, forward, sinogram)))
    count = lax.axis_size("ang")
    near = lax.ppermute(own, "ang", [(i, i ^ 1) for i in range(count)])
    far = lax.ppermute(far, "ang", [(i, (i + 1 if i % 2 else i - 1) % count) for i in range(count)])
    width = 3 * 4 * BLOCKS
    w1, w2, w3, col1, col2, pick = pl.pallas_call(
        layout_kernel,
        out_shape=(
            jax.ShapeDtypeStruct((ROWS1, 256), bf16),
            jax.ShapeDtypeStruct((GROUP2, 3 * GROUP1), bf16),
            jax.ShapeDtypeStruct((2, 24, 2 * GROUP2), f32),
            jax.ShapeDtypeStruct((CH, LANES), f32),
            jax.ShapeDtypeStruct((CH, LANES), f32),
            jax.ShapeDtypeStruct((SLABS_DEV * ROW_DEVS * SLAB_Z, width), bf16),
        ),
        out_specs=(vmem,) * 6,
        scratch_shapes=[
            pltpu.VMEM((32, LANES), f32),
            pltpu.VMEM((GROUP2, 3 * GROUP1), f32),
        ],
        compiler_params=pltpu.CompilerParams(vmem_limit_bytes=8 * MIB),
        name="layout_kernel",
    )(*map(in_hbm, (
        first_weight.transpose(0, 1, 3, 2).reshape(9, FIELDS, CH), middle_weight.reshape(9, CH, CH),
        last_weight.transpose(0, 2, 1, 3).reshape(3, 3, CH), first_bias[None], middle_bias[None],
        slab_order[None], offsets,
    )))
    work = [
        pltpu.VMEM((64, U), f32),
        pltpu.VMEM((256, U), bf16),
        pltpu.VMEM((ROWS_DEV, 3 * GROUP1, U), bf16),
        pltpu.VMEM((ROWS_DEV * GROUP2, U), bf16),
    ]
    shared, taps, ramp = pl.pallas_call(
        near_kernel,
        out_shape=(
            jax.ShapeDtypeStruct((ROWS_DEV, 3, 2 * CH, U), bf16),
            jax.ShapeDtypeStruct((24, U), f32),
            jax.ShapeDtypeStruct((2 * NBLK - 1, BLK, BLK), bf16),
        ),
        in_specs=[hbm] + [vmem] * 7,
        out_specs=(vmem,) * 3,
        scratch_shapes=work + [pltpu.SemaphoreType.DMA],
        compiler_params=pltpu.CompilerParams(vmem_limit_bytes=24 * MIB),
        name="near_kernel",
    )(in_hbm(ramp_tiles()), own, near, w1, w2, w3, col1, col2)
    new_dual, send = pl.pallas_call(
        far_kernel,
        out_shape=(
            jax.ShapeDtypeStruct((ANG_DEV, ROWS_DEV, U), bf16),
            jax.ShapeDtypeStruct((BLOCKS, 4, LANES), f32),
        ),
        in_specs=[hbm] * 3 + [vmem] * 10,
        out_specs=(hbm, vmem),
        scratch_shapes=work + [
            pltpu.VMEM((ANG_DEV, ROWS_DEV, U), bf16),
            pltpu.SMEM((ANG_DEV,), f32),
            pltpu.SMEM((ANG_DEV,), f32),
            pltpu.SMEM((ANG_DEV,), f32),
            pltpu.SemaphoreType.DMA((4,)),
        ],
        compiler_params=pltpu.CompilerParams(vmem_limit_bytes=24 * MIB),
        name="far_kernel",
    )(
        *map(in_hbm, (magnify, detector_shift, row_fraction)),
        own, far, shared, taps, ramp, w1, w2, w3, col1, col2,
    )
    got = lax.all_to_all(send, "ang", 0, 0, tiled=True)
    placed = pl.pallas_call(
        place_kernel,
        out_shape=jax.ShapeDtypeStruct((SLABS_DEV * ROW_DEVS * SLAB_Z, LANES), f32),
        in_specs=[vmem, vmem],
        out_specs=vmem,
        compiler_params=pltpu.CompilerParams(vmem_limit_bytes=4 * MIB),
        name="place_kernel",
    )(pick, got.reshape(4 * BLOCKS, LANES))
    shares = lax.all_to_all(placed.reshape(ROW_DEVS, SLABS_DEV * SLAB_Z, LANES), "row", 0, 0, tiled=True)
    return new_dual, jnp.sum(shares, axis=0) * 0.125


def solution(mesh):
    field = P("ang", "row", None)
    return jax.shard_map(
        per_device,
        mesh=mesh,
        in_specs=(field, field, field) + (P(),) * 5 + (P("ang"),) * 3 + (P(), P()),
        out_specs=(field, P("row", "ang")),
        check_vma=False,
    )
```

```python
import math

import jax
import jax.numpy as jnp
import numpy as np
from jax import lax
from jax.experimental import pallas as pl
from jax.experimental.pallas import tpu as pltpu
from jax.sharding import PartitionSpec as P

U = 2048
CH = 32
ANG_DEV = 4
ROWS_DEV = 2
HALO = 3
FIELDS = 3
SLAB_Z = 4
SLABS_DEV = 4
BLOCKS = 16
ROW_DEVS = 16
LANES = 128
TILES = U // LANES
BLK = 256
NBLK = U // BLK
SPAN = ANG_DEV + 2 * HALO
ROWS1 = ROWS_DEV * (SPAN - 2) * CH
HALF1 = (SPAN - 2) * CH
GROUP1 = 5 * CH
GROUP2 = 3 * CH
OUT8 = ANG_DEV * ROWS_DEV
CENTRE = (U - 1) / 2.0
MIB = 1024 * 1024
MAG_LOW, MAG_HIGH, SHIFT_MAX = 0.85, 0.95, 8.0


def ramp_tiles():
    row_ids = np.arange(BLK, dtype=np.int32)[None, :, None]
    col_ids = np.arange(BLK, dtype=np.int32)[None, None, :]
    gaps = np.arange(-(NBLK - 1), NBLK, dtype=np.int32)[:, None, None] * BLK
    diff = row_ids - (col_ids + gaps)
    odd = np.abs(diff) % 2 == 1
    distance = np.where(odd, diff, 1).astype(np.float32)
    falloff = np.float32(-1.0) / (np.float32(math.pi * math.pi) * distance * distance)
    tiles = np.where(diff == 0, np.float32(0.25), np.where(odd, falloff, np.float32(0.0)))
    return jnp.asarray(tiles.astype(np.float32)).astype(jnp.bfloat16)


def shifted(value, step):
    lane = lax.broadcasted_iota(jnp.int32, value.shape, 1)
    if step < 0:
        return jnp.where(lane == 0, 0.0, pltpu.roll(value, 1, 1))
    return jnp.where(lane == U - 1, 0.0, pltpu.roll(value, U - 1, 1))


def silu(value):
    half = 0.5 * value
    return half + half * jnp.tanh(half)


def source_tiles(tile):
    ends = []
    for column in (tile * LANES, tile * LANES + LANES - 1):
        for mag in (MAG_LOW, MAG_HIGH):
            for shift in (-SHIFT_MAX, SHIFT_MAX):
                ends.append((column - CENTRE) * mag + CENTRE + shift)
    low = int(math.floor(min(ends) - 0.5))
    high = int(math.floor(max(ends) + 0.5)) + 1
    return max(low, 0) // LANES, min(high, U - 1) // LANES


def parity():
    return lax.axis_index("ang") % 2


def turned(index, last):
    return index + parity() * (last - 2 * index)


def pack_kernel(dual_hbm, forw_hbm, sino_hbm, own_ref, far_ref, sems):
    loads = []
    for at, field in enumerate((dual_hbm, forw_hbm, sino_hbm)):
        side = field.at[pl.ds(parity(), HALO)]
        loads.append(pltpu.make_async_copy(side, far_ref.at[pl.ds(at * HALO, HALO)], sems.at[at]))
        loads.append(pltpu.make_async_copy(field, own_ref.at[pl.ds(at * ANG_DEV, ANG_DEV)], sems.at[3 + at]))
    for load in loads:
        load.start()
    for load in loads:
        load.wait()


def layout_kernel(
    first_ref, middle_ref, last_ref, bias1_ref, bias2_ref, order_ref, offs_ref, mag_ref, move_ref, frac_ref,
    w1_ref, w2_ref, w3_ref, col1_ref, col2_ref, pick_ref, angle_ref,
    gather1, base2,
):
    f32, bf16 = jnp.float32, jnp.bfloat16
    gather1[...] = jnp.zeros(gather1.shape, f32)
    for ang_tap in range(3):
        for tap in range(3):
            part = 3 * ang_tap + tap
            gather1[3 * part:3 * part + 3, 0:CH] = first_ref[3 * turned(ang_tap, 2) + tap].astype(f32)
    key = lax.broadcasted_iota(jnp.int32, (32, 256), 0)
    lane = lax.broadcasted_iota(jnp.int32, (32, 256), 1)
    wanted = (key // 3 % 3) * 64 + (key % 3) * (2 * SPAN) + (key // 9) * 2
    spread = jnp.where((lane == wanted) & (key < 27), 1.0, 0.0)
    base1 = lax.dot_general(
        gather1[...].astype(bf16), spread.astype(bf16), (((0,), (0,)), ((), ())), preferred_element_type=f32
    )[0:CH]
    for row in range(ROWS_DEV):
        for ang in range(SPAN - 2):
            shift = 2 * ang + row
            rolled = pltpu.roll(base1, shift, 1) if shift else base1
            start = (row * (SPAN - 2) + ang) * CH
            w1_ref[start:start + CH, :] = rolled.astype(bf16)
    base2[...] = jnp.zeros(base2.shape, f32)
    for ang_tap in range(3):
        for tap in range(3):
            block = middle_ref[3 * turned(ang_tap, 2) + tap].astype(f32)
            for ang in range(3):
                start = tap * GROUP1 + (ang + ang_tap) * CH
                base2[ang * CH:(ang + 1) * CH, start:start + CH] = block
    w2_ref[...] = base2[...].astype(bf16)
    w3_ref[...] = jnp.zeros(w3_ref.shape, f32)
    for ang_tap in range(3):
        block = last_ref[turned(ang_tap, 2)].astype(f32)
        for ang in range(ANG_DEV):
            source = ang + ang_tap
            for row in range(ROWS_DEV):
                start = row * GROUP2 + source % 3 * CH
                for tap in range(3):
                    at = tap * OUT8 + ang * ROWS_DEV + row
                    w3_ref[source // 3, at:at + 1, start:start + CH] = block[tap:tap + 1, :]
    square = (CH, CH)
    eye = lax.broadcasted_iota(jnp.int32, square, 0) == lax.broadcasted_iota(jnp.int32, square, 1)
    for bias_ref, col_ref in ((bias1_ref, col1_ref), (bias2_ref, col2_ref)):
        column = jnp.sum(jnp.where(eye, jnp.broadcast_to(bias_ref[...], square), 0.0), axis=1, keepdims=True)
        col_ref[...] = jnp.broadcast_to(column, (CH, LANES))
    ang = lax.broadcasted_iota(jnp.int32, (OUT8, ANG_DEV), 0) // ROWS_DEV
    mine = lax.broadcasted_iota(jnp.int32, (OUT8, ANG_DEV), 1) == turned(ang, ANG_DEV - 1)
    for at, ref in enumerate((mag_ref, move_ref, frac_ref)):
        value = jnp.sum(jnp.where(mine, jnp.broadcast_to(ref[...], (OUT8, ANG_DEV)), 0.0), axis=1, keepdims=True)
        angle_ref[at] = jnp.broadcast_to(value, (OUT8, LANES))
    slabs = SLABS_DEV * ROW_DEVS
    chosen = jnp.broadcast_to(order_ref[...], (slabs, slabs)) == lax.broadcasted_iota(jnp.int32, (slabs, slabs), 0)
    chosen = jnp.where(chosen, 1.0, 0.0).astype(bf16)
    starts = jnp.dot(offs_ref[...].astype(f32).astype(bf16), chosen, preferred_element_type=f32)
    width = 3 * 4 * BLOCKS
    block_of = (lax.broadcasted_iota(jnp.int32, (BLOCKS, width), 1) % (4 * BLOCKS)) // 4
    widen = jnp.where(block_of == lax.broadcasted_iota(jnp.int32, (BLOCKS, width), 0), 1.0, 0.0).astype(bf16)
    starts = lax.dot_general(
        starts.astype(bf16), widen, (((0,), (0,)), ((), ())), preferred_element_type=f32
    )
    rows = slabs * SLAB_Z
    slot_of = lax.broadcasted_iota(jnp.int32, (rows, slabs), 0) // SLAB_Z
    tall = jnp.where(slot_of == lax.broadcasted_iota(jnp.int32, (rows, slabs), 1), 1.0, 0.0).astype(bf16)
    starts = jnp.dot(tall, starts.astype(bf16), preferred_element_type=f32)
    depth = lax.broadcasted_iota(jnp.int32, (rows, width), 0) % SLAB_Z
    kind = lax.broadcasted_iota(jnp.int32, (rows, width), 1) % 4
    offset = depth + kind // 2 - kind % 2 - ROWS_DEV * lax.axis_index("row")
    pick_ref[...] = jnp.where(starts + offset.astype(f32) == 0.0, 1.0, 0.0).astype(bf16)


def lay_inputs(x32, xcat, own_ref, side_ref, side, sent):
    f32, bf16 = jnp.float32, jnp.bfloat16
    x32[...] = jnp.zeros(x32.shape, f32)
    for field in range(FIELDS):
        base = field * 2 * SPAN
        for ang in range(ANG_DEV):
            at = base + 2 * (HALO + ang)
            x32[at:at + 2, :] = own_ref[field * ANG_DEV + turned(ang, ANG_DEV - 1)].astype(f32)
        for ang in range(HALO):
            at = base + 2 * (side + ang)
            x32[at:at + 2, :] = side_ref[field * sent + turned(ang, sent - 1)].astype(f32)
    stacked = x32[...]
    xcat[0:64, :] = shifted(stacked, -1).astype(bf16)
    xcat[64:128, :] = stacked.astype(bf16)
    xcat[128:192, :] = shifted(stacked, 1).astype(bf16)
    xcat[192:256, :] = jnp.zeros((64, U), bf16)


def first_layer(xcat, w1_ref, bias1, act1, row, first, count):
    f32, bf16 = jnp.float32, jnp.bfloat16
    start, size = row * HALF1 + first * CH, count * CH
    lane = lax.broadcasted_iota(jnp.int32, (size, LANES), 1)
    nothing = jnp.zeros((size, LANES), bf16)
    before_edge, after_rest = nothing, None
    for step in range(NBLK):
        cols = slice(step * BLK, (step + 1) * BLK)
        block = jnp.dot(w1_ref[start:start + size, :], xcat[:, cols], preferred_element_type=f32)
        act = jnp.concatenate(
            [silu(block[part * CH:(part + 1) * CH] + bias1) for part in range(count)], axis=0
        ).astype(bf16)
        act1[row, GROUP1:GROUP1 + size, cols] = act
        before = pltpu.roll(act, 1, 1)
        act1[row, 0:size, step * BLK:step * BLK + LANES] = jnp.where(lane == 0, before_edge, before[:, 0:LANES])
        act1[row, 0:size, step * BLK + LANES:(step + 1) * BLK] = before[:, LANES:]
        before_edge = before[:, 0:LANES]
        after = pltpu.roll(act, BLK - 1, 1)
        act1[row, 2 * GROUP1:2 * GROUP1 + size, step * BLK:step * BLK + LANES] = after[:, 0:LANES]
        if step:
            act1[row, 2 * GROUP1:2 * GROUP1 + size, step * BLK - LANES:step * BLK] = jnp.where(
                lane == LANES - 1, after[:, LANES:], after_rest
            )
        after_rest = after[:, LANES:]
    act1[row, 2 * GROUP1:2 * GROUP1 + size, U - LANES:] = jnp.where(lane == LANES - 1, nothing, after_rest)


def first_layer_whole(xcat, w1_ref, bias1, act1, row, first, count):
    f32, bf16 = jnp.float32, jnp.bfloat16
    start = row * HALF1 + first * CH
    for step in range(NBLK):
        cols = slice(step * BLK, (step + 1) * BLK)
        block = jnp.dot(w1_ref[start:start + count * CH, :], xcat[:, cols], preferred_element_type=f32)
        for part in range(count):
            rows = slice(GROUP1 + part * CH, GROUP1 + (part + 1) * CH)
            act1[row, rows, cols] = silu(block[part * CH:(part + 1) * CH] + bias1).astype(bf16)
    edge = lax.broadcasted_iota(jnp.int32, (CH, LANES), 1)
    for part in range(count):
        low, middle, high = (slice(tap * GROUP1 + part * CH, tap * GROUP1 + (part + 1) * CH) for tap in range(3))
        here = act1[row, middle, :]
        before = pltpu.roll(here, 1, 1)
        after = pltpu.roll(here, U - 1, 1)
        act1[row, low, LANES:] = before[:, LANES:]
        act1[row, low, 0:LANES] = jnp.where(edge == 0, 0.0, before[:, 0:LANES].astype(f32)).astype(bf16)
        act1[row, high, 0:U - LANES] = after[:, 0:U - LANES]
        last = after[:, U - LANES:].astype(f32)
        act1[row, high, U - LANES:] = jnp.where(edge == LANES - 1, 0.0, last).astype(bf16)


def second_layer(w2_ref, bias2, act1, act2):
    f32, bf16 = jnp.float32, jnp.bfloat16
    for row in range(ROWS_DEV):
        for step in range(NBLK):
            cols = slice(step * BLK, (step + 1) * BLK)
            block = jnp.dot(w2_ref[...], act1[row, :, cols], preferred_element_type=f32)
            for part in range(3):
                rows = slice(row * GROUP2 + part * CH, row * GROUP2 + (part + 1) * CH)
                act2[rows, cols] = silu(block[part * CH:(part + 1) * CH] + bias2).astype(bf16)


def near_kernel(
    ramp_hbm, own_ref, near_ref, w1_ref, w2_ref, w3_ref, col1_ref, col2_ref,
    shared_ref, taps_ref, ramp_ref,
    x32, xcat, act1, act2, sem,
):
    load = pltpu.make_async_copy(ramp_hbm, ramp_ref, sem)
    load.start()
    bias1, bias2 = col1_ref[:, 0:1], col2_ref[:, 0:1]
    lay_inputs(x32, xcat, own_ref, near_ref, HALO + ANG_DEV, ANG_DEV)
    for row in range(ROWS_DEV):
        first_layer_whole(xcat, w1_ref, bias1, act1, row, 3, 5)
        for tap in range(3):
            shared_ref[row, tap] = act1[row, tap * GROUP1:tap * GROUP1 + 2 * CH, :]
    second_layer(w2_ref, bias2, act1, act2)
    taps_ref[...] = jnp.dot(w3_ref[1].astype(jnp.bfloat16), act2[...], preferred_element_type=jnp.float32)
    load.wait()


def far_kernel(
    angle_ref, own_ref, far_ref, shared_ref, taps_ref, ramp_ref,
    w1_ref, w2_ref, w3_ref, col1_ref, col2_ref,
    dual_hbm, send_ref,
    x32, xcat, act1, act2, dual_ref, sem,
):
    f32, bf16 = jnp.float32, jnp.bfloat16
    bias1, bias2 = col1_ref[:, 0:1], col2_ref[:, 0:1]
    lay_inputs(x32, xcat, own_ref, far_ref, 0, HALO)
    for row in range(ROWS_DEV):
        first_layer(xcat, w1_ref, bias1, act1, row, 0, 3)
        for tap in range(3):
            act1[row, tap * GROUP1 + 3 * CH:(tap + 1) * GROUP1, :] = shared_ref[row, tap]
    second_layer(w2_ref, bias2, act1, act2)
    taps3 = taps_ref[...] + jnp.dot(w3_ref[0].astype(bf16), act2[...], preferred_element_type=f32)
    update = shifted(taps3[0:8], -1) + taps3[8:16] + shifted(taps3[16:24], 1)
    own_dual = x32[2 * HALO:2 * HALO + OUT8, :]
    new_dual = (own_dual + update).astype(bf16)
    for ang in range(ANG_DEV):
        dual_ref[turned(ang, ANG_DEV - 1)] = new_dual[2 * ang:2 * ang + 2, :]
    store = pltpu.make_async_copy(dual_ref, dual_hbm, sem)
    store.start()
    dual32 = new_dual.astype(f32)
    blocks = jnp.concatenate([dual32[:, b * BLK:(b + 1) * BLK] for b in range(NBLK)], axis=0).astype(bf16)
    filtered = [None] * NBLK
    for gap in range(-(NBLK - 1), NBLK):
        part = jnp.dot(blocks, ramp_ref[gap + NBLK - 1], preferred_element_type=f32)
        for source in range(NBLK):
            target = source + gap
            if 0 <= target < NBLK:
                piece = part[source * OUT8:(source + 1) * OUT8]
                filtered[target] = piece if filtered[target] is None else filtered[target] + piece
    lanes = [filtered[t // 2][:, (t % 2) * LANES:(t % 2 + 1) * LANES] for t in range(TILES)]
    row_id = lax.broadcasted_iota(jnp.int32, (OUT8, LANES), 0)
    lane_id = lax.broadcasted_iota(jnp.int32, (OUT8, LANES), 1)
    mag, move, frac = angle_ref[0], angle_ref[1], angle_ref[2]
    keep = 1.0 - frac
    for tile in range(TILES):
        column = (lane_id + tile * LANES).astype(f32)
        place = (column - CENTRE) * mag + CENTRE + move
        floor = jnp.floor(place)
        weight = place - floor
        low = floor.astype(jnp.int32)
        high = low + 1
        first, last = source_tiles(tile)
        left = jnp.zeros((OUT8, LANES), f32)
        right = jnp.zeros((OUT8, LANES), f32)
        for source in range(first, last + 1):
            got = jnp.take_along_axis(lanes[source], low & (LANES - 1), axis=1, mode="promise_in_bounds")
            left = jnp.where(low // LANES == source, got, left)
            got = jnp.take_along_axis(lanes[source], high & (LANES - 1), axis=1, mode="promise_in_bounds")
            right = jnp.where(high // LANES == source, got, right)
        projected = ((1.0 - weight) * left + weight * right).astype(bf16).astype(f32)
        lower = keep * projected
        upper = frac * projected
        lower = lower + pltpu.roll(lower, 4, 0)
        lower = lower + pltpu.roll(lower, 2, 0)
        upper = upper + pltpu.roll(upper, 4, 0)
        upper = upper + pltpu.roll(upper, 2, 0)
        packed = jnp.where(row_id < ROWS_DEV, lower, upper)
        send_ref[tile] = packed[0:4]
    store.wait()


def place_kernel(pick_ref, got_ref, out_ref):
    f32, bf16 = jnp.float32, jnp.bfloat16
    rows = got_ref[...]
    high = rows.astype(bf16)
    rest = rows - high.astype(f32)
    mid = rest.astype(bf16)
    low = (rest - mid.astype(f32)).astype(bf16)
    parts = jnp.concatenate([high, mid, low], axis=0)
    out_ref[...] = jnp.dot(pick_ref[...], parts, preferred_element_type=f32)


def in_hbm(value):
    return pltpu.with_memory_space_constraint(value, pltpu.HBM)


def per_device(
    dual_field, forward, sinogram, first_weight, first_bias, middle_weight, middle_bias, last_weight,
    magnify, detector_shift, row_fraction, offsets, slab_order,
):
    f32, bf16 = jnp.float32, jnp.bfloat16
    vmem = pl.BlockSpec(memory_space=pltpu.VMEM)
    hbm = pl.BlockSpec(memory_space=pltpu.HBM)
    own, far = pl.pallas_call(
        pack_kernel,
        out_shape=(
            jax.ShapeDtypeStruct((FIELDS * ANG_DEV, ROWS_DEV, U), bf16),
            jax.ShapeDtypeStruct((FIELDS * HALO, ROWS_DEV, U), bf16),
        ),
        in_specs=[hbm] * 3,
        out_specs=(vmem,) * 2,
        scratch_shapes=[pltpu.SemaphoreType.DMA((6,))],
        compiler_params=pltpu.CompilerParams(vmem_limit_bytes=2 * MIB),
        name="pack_kernel",
    )(*map(in_hbm, (dual_field, forward, sinogram)))
    count = lax.axis_size("ang")
    near = lax.ppermute(own, "ang", [(i, i ^ 1) for i in range(count)])
    far = lax.ppermute(far, "ang", [(i, (i + 1 if i % 2 else i - 1) % count) for i in range(count)])
    width = 3 * 4 * BLOCKS
    w1, w2, w3, col1, col2, pick, angles = pl.pallas_call(
        layout_kernel,
        out_shape=(
            jax.ShapeDtypeStruct((ROWS1, 256), bf16),
            jax.ShapeDtypeStruct((GROUP2, 3 * GROUP1), bf16),
            jax.ShapeDtypeStruct((2, 24, 2 * GROUP2), f32),
            jax.ShapeDtypeStruct((CH, LANES), f32),
            jax.ShapeDtypeStruct((CH, LANES), f32),
            jax.ShapeDtypeStruct((SLABS_DEV * ROW_DEVS * SLAB_Z, width), bf16),
            jax.ShapeDtypeStruct((3, OUT8, LANES), f32),
        ),
        out_specs=(vmem,) * 7,
        scratch_shapes=[
            pltpu.VMEM((32, LANES), f32),
            pltpu.VMEM((GROUP2, 3 * GROUP1), f32),
        ],
        compiler_params=pltpu.CompilerParams(vmem_limit_bytes=8 * MIB),
        name="layout_kernel",
    )(*map(in_hbm, (
        first_weight.transpose(0, 1, 3, 2).reshape(9, FIELDS, CH), middle_weight.reshape(9, CH, CH),
        last_weight.transpose(0, 2, 1, 3).reshape(3, 3, CH), first_bias[None], middle_bias[None],
        slab_order[None], offsets, magnify[None], detector_shift[None], row_fraction[None],
    )))
    work = [
        pltpu.VMEM((64, U), f32),
        pltpu.VMEM((256, U), bf16),
        pltpu.VMEM((ROWS_DEV, 3 * GROUP1, U), bf16),
        pltpu.VMEM((ROWS_DEV * GROUP2, U), bf16),
    ]
    shared, taps, ramp = pl.pallas_call(
        near_kernel,
        out_shape=(
            jax.ShapeDtypeStruct((ROWS_DEV, 3, 2 * CH, U), bf16),
            jax.ShapeDtypeStruct((24, U), f32),
            jax.ShapeDtypeStruct((2 * NBLK - 1, BLK, BLK), bf16),
        ),
        in_specs=[hbm] + [vmem] * 7,
        out_specs=(vmem,) * 3,
        scratch_shapes=work + [pltpu.SemaphoreType.DMA],
        compiler_params=pltpu.CompilerParams(vmem_limit_bytes=24 * MIB),
        name="near_kernel",
    )(in_hbm(ramp_tiles()), own, near, w1, w2, w3, col1, col2)
    new_dual, send = pl.pallas_call(
        far_kernel,
        out_shape=(
            jax.ShapeDtypeStruct((ANG_DEV, ROWS_DEV, U), bf16),
            jax.ShapeDtypeStruct((BLOCKS, 4, LANES), f32),
        ),
        in_specs=[vmem] * 11,
        out_specs=(hbm, vmem),
        scratch_shapes=work + [
            pltpu.VMEM((ANG_DEV, ROWS_DEV, U), bf16),
            pltpu.SemaphoreType.DMA,
        ],
        compiler_params=pltpu.CompilerParams(vmem_limit_bytes=24 * MIB),
        name="far_kernel",
    )(angles, own, far, shared, taps, ramp, w1, w2, w3, col1, col2)
    got = lax.all_to_all(send, "ang", 0, 0, tiled=True)
    placed = pl.pallas_call(
        place_kernel,
        out_shape=jax.ShapeDtypeStruct((SLABS_DEV * ROW_DEVS * SLAB_Z, LANES), f32),
        in_specs=[vmem, vmem],
        out_specs=vmem,
        compiler_params=pltpu.CompilerParams(vmem_limit_bytes=4 * MIB),
        name="place_kernel",
    )(pick, got.reshape(4 * BLOCKS, LANES))
    shares = lax.all_to_all(placed.reshape(ROW_DEVS, SLABS_DEV * SLAB_Z, LANES), "row", 0, 0, tiled=True)
    return new_dual, jnp.sum(shares, axis=0) * 0.125


def solution(mesh):
    field = P("ang", "row", None)
    return jax.shard_map(
        per_device,
        mesh=mesh,
        in_specs=(field, field, field) + (P(),) * 5 + (P("ang"),) * 3 + (P(), P()),
        out_specs=(field, P("row", "ang")),
        check_vma=False,
    )
```

```python
import math

import jax
import jax.numpy as jnp
import numpy as np
from jax import lax
from jax.experimental import pallas as pl
from jax.experimental.pallas import tpu as pltpu
from jax.sharding import PartitionSpec as P

U = 2048
CH = 32
ANG_DEV = 4
ROWS_DEV = 2
HALO = 3
FIELDS = 3
SLAB_Z = 4
SLABS_DEV = 4
BLOCKS = 16
ROW_DEVS = 16
LANES = 128
TILES = U // LANES
BLK = 256
NBLK = U // BLK
SPAN = ANG_DEV + 2 * HALO
ROWS1 = ROWS_DEV * (SPAN - 2) * CH
HALF1 = (SPAN - 2) * CH
GROUP1 = 5 * CH
GROUP2 = 3 * CH
OUT8 = ANG_DEV * ROWS_DEV
CENTRE = (U - 1) / 2.0
MIB = 1024 * 1024
MAG_LOW, MAG_HIGH, SHIFT_MAX = 0.85, 0.95, 8.0


def ramp_tiles():
    row_ids = np.arange(BLK, dtype=np.int32)[None, :, None]
    col_ids = np.arange(BLK, dtype=np.int32)[None, None, :]
    gaps = np.arange(-(NBLK - 1), NBLK, dtype=np.int32)[:, None, None] * BLK
    diff = row_ids - (col_ids + gaps)
    odd = np.abs(diff) % 2 == 1
    distance = np.where(odd, diff, 1).astype(np.float32)
    falloff = np.float32(-1.0) / (np.float32(math.pi * math.pi) * distance * distance)
    tiles = np.where(diff == 0, np.float32(0.25), np.where(odd, falloff, np.float32(0.0)))
    return jnp.asarray(tiles.astype(np.float32)).astype(jnp.bfloat16)


def shifted(value, step):
    lane = lax.broadcasted_iota(jnp.int32, value.shape, 1)
    if step < 0:
        return jnp.where(lane == 0, 0.0, pltpu.roll(value, 1, 1))
    return jnp.where(lane == U - 1, 0.0, pltpu.roll(value, U - 1, 1))


def silu(value):
    half = 0.5 * value
    return half + half * jnp.tanh(half)


def source_tiles(tile):
    ends = []
    for column in (tile * LANES, tile * LANES + LANES - 1):
        for mag in (MAG_LOW, MAG_HIGH):
            for shift in (-SHIFT_MAX, SHIFT_MAX):
                ends.append((column - CENTRE) * mag + CENTRE + shift)
    low = int(math.floor(min(ends) - 0.5))
    high = int(math.floor(max(ends) + 0.5)) + 1
    return max(low, 0) // LANES, min(high, U - 1) // LANES


def parity():
    return lax.axis_index("ang") % 2


def turned(index, last):
    return index + parity() * (last - 2 * index)


def pack_kernel(dual_hbm, forw_hbm, sino_hbm, own_ref, far_ref, sems):
    loads = []
    for at, field in enumerate((dual_hbm, forw_hbm, sino_hbm)):
        side = field.at[pl.ds(parity(), HALO)]
        loads.append(pltpu.make_async_copy(side, far_ref.at[pl.ds(at * HALO, HALO)], sems.at[at]))
        loads.append(pltpu.make_async_copy(field, own_ref.at[pl.ds(at * ANG_DEV, ANG_DEV)], sems.at[3 + at]))
    for load in loads:
        load.start()
    for load in loads:
        load.wait()


def layout_kernel(
    first_ref, middle_ref, last_ref, bias1_ref, bias2_ref, order_ref, offs_ref, mag_ref, move_ref, frac_ref,
    w1_ref, w2_ref, w3_ref, col1_ref, col2_ref, pick_ref, angle_ref,
    gather1, base2,
):
    f32, bf16 = jnp.float32, jnp.bfloat16
    gather1[...] = jnp.zeros(gather1.shape, f32)
    for ang_tap in range(3):
        for tap in range(3):
            part = 3 * ang_tap + tap
            gather1[3 * part:3 * part + 3, 0:CH] = first_ref[3 * turned(ang_tap, 2) + tap].astype(f32)
    key = lax.broadcasted_iota(jnp.int32, (32, 256), 0)
    lane = lax.broadcasted_iota(jnp.int32, (32, 256), 1)
    wanted = (key // 3 % 3) * 64 + (key % 3) * (2 * SPAN) + (key // 9) * 2
    spread = jnp.where((lane == wanted) & (key < 27), 1.0, 0.0)
    base1 = lax.dot_general(
        gather1[...].astype(bf16), spread.astype(bf16), (((0,), (0,)), ((), ())), preferred_element_type=f32
    )[0:CH]
    for row in range(ROWS_DEV):
        for ang in range(SPAN - 2):
            shift = 2 * ang + row
            rolled = pltpu.roll(base1, shift, 1) if shift else base1
            start = (row * (SPAN - 2) + ang) * CH
            w1_ref[start:start + CH, :] = rolled[:, 0:192].astype(bf16)
    base2[...] = jnp.zeros(base2.shape, f32)
    for ang_tap in range(3):
        for tap in range(3):
            block = middle_ref[3 * turned(ang_tap, 2) + tap].astype(f32)
            for ang in range(3):
                start = tap * GROUP1 + (ang + ang_tap) * CH
                base2[ang * CH:(ang + 1) * CH, start:start + CH] = block
    w2_ref[...] = base2[...].astype(bf16)
    w3_ref[...] = jnp.zeros(w3_ref.shape, f32)
    for ang_tap in range(3):
        block = last_ref[turned(ang_tap, 2)].astype(f32)
        for ang in range(ANG_DEV):
            source = ang + ang_tap
            for row in range(ROWS_DEV):
                start = row * GROUP2 + source % 3 * CH
                for tap in range(3):
                    at = tap * OUT8 + ang * ROWS_DEV + row
                    w3_ref[source // 3, at:at + 1, start:start + CH] = block[tap:tap + 1, :]
    square = (CH, CH)
    eye = lax.broadcasted_iota(jnp.int32, square, 0) == lax.broadcasted_iota(jnp.int32, square, 1)
    for bias_ref, col_ref in ((bias1_ref, col1_ref), (bias2_ref, col2_ref)):
        column = jnp.sum(jnp.where(eye, jnp.broadcast_to(bias_ref[...], square), 0.0), axis=1, keepdims=True)
        col_ref[...] = jnp.broadcast_to(column, (CH, LANES))
    ang = lax.broadcasted_iota(jnp.int32, (OUT8, ANG_DEV), 0) // ROWS_DEV
    mine = lax.broadcasted_iota(jnp.int32, (OUT8, ANG_DEV), 1) == turned(ang, ANG_DEV - 1)
    for at, ref in enumerate((mag_ref, move_ref, frac_ref)):
        value = jnp.sum(jnp.where(mine, jnp.broadcast_to(ref[...], (OUT8, ANG_DEV)), 0.0), axis=1, keepdims=True)
        angle_ref[at] = jnp.broadcast_to(value, (OUT8, LANES))
    slabs = SLABS_DEV * ROW_DEVS
    chosen = jnp.broadcast_to(order_ref[...], (slabs, slabs)) == lax.broadcasted_iota(jnp.int32, (slabs, slabs), 0)
    chosen = jnp.where(chosen, 1.0, 0.0).astype(bf16)
    starts = jnp.dot(offs_ref[...].astype(f32).astype(bf16), chosen, preferred_element_type=f32)
    width = 3 * 4 * BLOCKS
    block_of = (lax.broadcasted_iota(jnp.int32, (BLOCKS, width), 1) % (4 * BLOCKS)) // 4
    widen = jnp.where(block_of == lax.broadcasted_iota(jnp.int32, (BLOCKS, width), 0), 1.0, 0.0).astype(bf16)
    starts = lax.dot_general(
        starts.astype(bf16), widen, (((0,), (0,)), ((), ())), preferred_element_type=f32
    )
    rows = slabs * SLAB_Z
    slot_of = lax.broadcasted_iota(jnp.int32, (rows, slabs), 0) // SLAB_Z
    tall = jnp.where(slot_of == lax.broadcasted_iota(jnp.int32, (rows, slabs), 1), 1.0, 0.0).astype(bf16)
    starts = jnp.dot(tall, starts.astype(bf16), preferred_element_type=f32)
    depth = lax.broadcasted_iota(jnp.int32, (rows, width), 0) % SLAB_Z
    kind = lax.broadcasted_iota(jnp.int32, (rows, width), 1) % 4
    offset = depth + kind // 2 - kind % 2 - ROWS_DEV * lax.axis_index("row")
    pick_ref[...] = jnp.where(starts + offset.astype(f32) == 0.0, 0.125, 0.0).astype(bf16)


def lay_inputs(x32, xcat, own_ref, side_ref, side, sent):
    f32, bf16 = jnp.float32, jnp.bfloat16
    x32[...] = jnp.zeros(x32.shape, f32)
    for field in range(FIELDS):
        base = field * 2 * SPAN
        for ang in range(ANG_DEV):
            at = base + 2 * (HALO + ang)
            x32[at:at + 2, :] = own_ref[field * ANG_DEV + turned(ang, ANG_DEV - 1)].astype(f32)
        for ang in range(HALO):
            at = base + 2 * (side + ang)
            x32[at:at + 2, :] = side_ref[field * sent + turned(ang, sent - 1)].astype(f32)
    stacked = x32[...]
    xcat[0:64, :] = shifted(stacked, -1).astype(bf16)
    xcat[64:128, :] = stacked.astype(bf16)
    xcat[128:192, :] = shifted(stacked, 1).astype(bf16)


def first_layer(xcat, w1_ref, bias1, act1, row, first, count):
    f32, bf16 = jnp.float32, jnp.bfloat16
    start, size = row * HALF1 + first * CH, count * CH
    lane = lax.broadcasted_iota(jnp.int32, (size, LANES), 1)
    nothing = jnp.zeros((size, LANES), bf16)
    before_edge, after_rest = nothing, None
    for step in range(NBLK):
        cols = slice(step * BLK, (step + 1) * BLK)
        block = jnp.dot(w1_ref[start:start + size, :], xcat[:, cols], preferred_element_type=f32)
        act = jnp.concatenate(
            [silu(block[part * CH:(part + 1) * CH] + bias1) for part in range(count)], axis=0
        ).astype(bf16)
        act1[row, GROUP1:GROUP1 + size, cols] = act
        before = pltpu.roll(act, 1, 1)
        act1[row, 0:size, step * BLK:step * BLK + LANES] = jnp.where(lane == 0, before_edge, before[:, 0:LANES])
        act1[row, 0:size, step * BLK + LANES:(step + 1) * BLK] = before[:, LANES:]
        before_edge = before[:, 0:LANES]
        after = pltpu.roll(act, BLK - 1, 1)
        act1[row, 2 * GROUP1:2 * GROUP1 + size, step * BLK:step * BLK + LANES] = after[:, 0:LANES]
        if step:
            act1[row, 2 * GROUP1:2 * GROUP1 + size, step * BLK - LANES:step * BLK] = jnp.where(
                lane == LANES - 1, after[:, LANES:], after_rest
            )
        after_rest = after[:, LANES:]
    act1[row, 2 * GROUP1:2 * GROUP1 + size, U - LANES:] = jnp.where(lane == LANES - 1, nothing, after_rest)


def first_layer_whole(xcat, w1_ref, bias1, act1, row, first, count):
    f32, bf16 = jnp.float32, jnp.bfloat16
    start = row * HALF1 + first * CH
    for step in range(NBLK):
        cols = slice(step * BLK, (step + 1) * BLK)
        block = jnp.dot(w1_ref[start:start + count * CH, :], xcat[:, cols], preferred_element_type=f32)
        for part in range(count):
            rows = slice(GROUP1 + part * CH, GROUP1 + (part + 1) * CH)
            act1[row, rows, cols] = silu(block[part * CH:(part + 1) * CH] + bias1).astype(bf16)
    edge = lax.broadcasted_iota(jnp.int32, (CH, LANES), 1)
    for part in range(count):
        low, middle, high = (slice(tap * GROUP1 + part * CH, tap * GROUP1 + (part + 1) * CH) for tap in range(3))
        here = act1[row, middle, :]
        before = pltpu.roll(here, 1, 1)
        after = pltpu.roll(here, U - 1, 1)
        act1[row, low, LANES:] = before[:, LANES:]
        act1[row, low, 0:LANES] = jnp.where(edge == 0, 0.0, before[:, 0:LANES].astype(f32)).astype(bf16)
        act1[row, high, 0:U - LANES] = after[:, 0:U - LANES]
        last = after[:, U - LANES:].astype(f32)
        act1[row, high, U - LANES:] = jnp.where(edge == LANES - 1, 0.0, last).astype(bf16)


def second_layer(w2_ref, bias2, act1, act2):
    f32, bf16 = jnp.float32, jnp.bfloat16
    for row in range(ROWS_DEV):
        for step in range(NBLK):
            cols = slice(step * BLK, (step + 1) * BLK)
            block = jnp.dot(w2_ref[...], act1[row, :, cols], preferred_element_type=f32)
            for part in range(3):
                rows = slice(row * GROUP2 + part * CH, row * GROUP2 + (part + 1) * CH)
                act2[rows, cols] = silu(block[part * CH:(part + 1) * CH] + bias2).astype(bf16)


def near_kernel(
    ramp_hbm, own_ref, near_ref, w1_ref, w2_ref, w3_ref, col1_ref, col2_ref,
    shared_ref, taps_ref, ramp_ref,
    x32, xcat, act1, act2, sem,
):
    load = pltpu.make_async_copy(ramp_hbm, ramp_ref, sem)
    load.start()
    bias1, bias2 = col1_ref[:, 0:1], col2_ref[:, 0:1]
    lay_inputs(x32, xcat, own_ref, near_ref, HALO + ANG_DEV, ANG_DEV)
    for row in range(ROWS_DEV):
        first_layer_whole(xcat, w1_ref, bias1, act1, row, 3, 5)
        for tap in range(3):
            shared_ref[row, tap] = act1[row, tap * GROUP1:tap * GROUP1 + 2 * CH, :]
    second_layer(w2_ref, bias2, act1, act2)
    taps_ref[...] = jnp.dot(w3_ref[1].astype(jnp.bfloat16), act2[...], preferred_element_type=jnp.float32)
    load.wait()


def far_kernel(
    angle_ref, own_ref, far_ref, shared_ref, taps_ref, ramp_ref,
    w1_ref, w2_ref, w3_ref, col1_ref, col2_ref,
    dual_hbm, send_ref,
    x32, xcat, act1, act2, dual_ref, sem,
):
    f32, bf16 = jnp.float32, jnp.bfloat16
    bias1, bias2 = col1_ref[:, 0:1], col2_ref[:, 0:1]
    lay_inputs(x32, xcat, own_ref, far_ref, 0, HALO)
    for row in range(ROWS_DEV):
        first_layer(xcat, w1_ref, bias1, act1, row, 0, 3)
        for tap in range(3):
            act1[row, tap * GROUP1 + 3 * CH:(tap + 1) * GROUP1, :] = shared_ref[row, tap]
    second_layer(w2_ref, bias2, act1, act2)
    taps3 = taps_ref[...] + jnp.dot(w3_ref[0].astype(bf16), act2[...], preferred_element_type=f32)
    update = shifted(taps3[0:8], -1) + taps3[8:16] + shifted(taps3[16:24], 1)
    own_dual = x32[2 * HALO:2 * HALO + OUT8, :]
    new_dual = (own_dual + update).astype(bf16)
    for ang in range(ANG_DEV):
        dual_ref[turned(ang, ANG_DEV - 1)] = new_dual[2 * ang:2 * ang + 2, :]
    store = pltpu.make_async_copy(dual_ref, dual_hbm, sem)
    store.start()
    dual32 = new_dual.astype(f32)
    blocks = jnp.concatenate([dual32[:, b * BLK:(b + 1) * BLK] for b in range(NBLK)], axis=0).astype(bf16)
    filtered = [None] * NBLK
    for gap in range(-(NBLK - 1), NBLK):
        part = jnp.dot(blocks, ramp_ref[gap + NBLK - 1], preferred_element_type=f32)
        for source in range(NBLK):
            target = source + gap
            if 0 <= target < NBLK:
                piece = part[source * OUT8:(source + 1) * OUT8]
                filtered[target] = piece if filtered[target] is None else filtered[target] + piece
    lanes = [filtered[t // 2][:, (t % 2) * LANES:(t % 2 + 1) * LANES] for t in range(TILES)]
    row_id = lax.broadcasted_iota(jnp.int32, (OUT8, LANES), 0)
    lane_id = lax.broadcasted_iota(jnp.int32, (OUT8, LANES), 1)
    mag, move, frac = angle_ref[0], angle_ref[1], angle_ref[2]
    keep = 1.0 - frac
    for tile in range(TILES):
        column = (lane_id + tile * LANES).astype(f32)
        place = (column - CENTRE) * mag + CENTRE + move
        floor = jnp.floor(place)
        weight = place - floor
        low = floor.astype(jnp.int32)
        high = low + 1
        first, last = source_tiles(tile)
        left = jnp.zeros((OUT8, LANES), f32)
        right = jnp.zeros((OUT8, LANES), f32)
        for source in range(first, last + 1):
            got = jnp.take_along_axis(lanes[source], low & (LANES - 1), axis=1, mode="promise_in_bounds")
            left = jnp.where(low // LANES == source, got, left)
            got = jnp.take_along_axis(lanes[source], high & (LANES - 1), axis=1, mode="promise_in_bounds")
            right = jnp.where(high // LANES == source, got, right)
        projected = ((1.0 - weight) * left + weight * right).astype(bf16).astype(f32)
        lower = keep * projected
        upper = frac * projected
        lower = lower + pltpu.roll(lower, 4, 0)
        lower = lower + pltpu.roll(lower, 2, 0)
        upper = upper + pltpu.roll(upper, 4, 0)
        upper = upper + pltpu.roll(upper, 2, 0)
        packed = jnp.where(row_id < ROWS_DEV, lower, upper)
        send_ref[tile] = packed[0:4]
    store.wait()


def place_kernel(pick_ref, got_ref, out_ref):
    f32, bf16 = jnp.float32, jnp.bfloat16
    rows = got_ref[...]
    high = rows.astype(bf16)
    rest = rows - high.astype(f32)
    mid = rest.astype(bf16)
    low = (rest - mid.astype(f32)).astype(bf16)
    parts = jnp.concatenate([high, mid, low], axis=0)
    out_ref[...] = jnp.dot(pick_ref[...], parts, preferred_element_type=f32)


def in_hbm(value):
    return pltpu.with_memory_space_constraint(value, pltpu.HBM)


def per_device(
    dual_field, forward, sinogram, first_weight, first_bias, middle_weight, middle_bias, last_weight,
    magnify, detector_shift, row_fraction, offsets, slab_order,
):
    f32, bf16 = jnp.float32, jnp.bfloat16
    vmem = pl.BlockSpec(memory_space=pltpu.VMEM)
    hbm = pl.BlockSpec(memory_space=pltpu.HBM)
    own, far = pl.pallas_call(
        pack_kernel,
        out_shape=(
            jax.ShapeDtypeStruct((FIELDS * ANG_DEV, ROWS_DEV, U), bf16),
            jax.ShapeDtypeStruct((FIELDS * HALO, ROWS_DEV, U), bf16),
        ),
        in_specs=[hbm] * 3,
        out_specs=(vmem,) * 2,
        scratch_shapes=[pltpu.SemaphoreType.DMA((6,))],
        compiler_params=pltpu.CompilerParams(vmem_limit_bytes=2 * MIB),
        name="pack_kernel",
    )(*map(in_hbm, (dual_field, forward, sinogram)))
    count = lax.axis_size("ang")
    near = lax.ppermute(own, "ang", [(i, i ^ 1) for i in range(count)])
    far = lax.ppermute(far, "ang", [(i, (i + 1 if i % 2 else i - 1) % count) for i in range(count)])
    width = 3 * 4 * BLOCKS
    w1, w2, w3, col1, col2, pick, angles = pl.pallas_call(
        layout_kernel,
        out_shape=(
            jax.ShapeDtypeStruct((ROWS1, 192), bf16),
            jax.ShapeDtypeStruct((GROUP2, 3 * GROUP1), bf16),
            jax.ShapeDtypeStruct((2, 24, 2 * GROUP2), f32),
            jax.ShapeDtypeStruct((CH, LANES), f32),
            jax.ShapeDtypeStruct((CH, LANES), f32),
            jax.ShapeDtypeStruct((SLABS_DEV * ROW_DEVS * SLAB_Z, width), bf16),
            jax.ShapeDtypeStruct((3, OUT8, LANES), f32),
        ),
        out_specs=(vmem,) * 7,
        scratch_shapes=[
            pltpu.VMEM((32, LANES), f32),
            pltpu.VMEM((GROUP2, 3 * GROUP1), f32),
        ],
        compiler_params=pltpu.CompilerParams(vmem_limit_bytes=8 * MIB),
        name="layout_kernel",
    )(*map(in_hbm, (
        first_weight.transpose(0, 1, 3, 2).reshape(9, FIELDS, CH), middle_weight.reshape(9, CH, CH),
        last_weight.transpose(0, 2, 1, 3).reshape(3, 3, CH), first_bias[None], middle_bias[None],
        slab_order[None], offsets, magnify[None], detector_shift[None], row_fraction[None],
    )))
    work = [
        pltpu.VMEM((64, U), f32),
        pltpu.VMEM((192, U), bf16),
        pltpu.VMEM((ROWS_DEV, 3 * GROUP1, U), bf16),
        pltpu.VMEM((ROWS_DEV * GROUP2, U), bf16),
    ]
    shared, taps, ramp = pl.pallas_call(
        near_kernel,
        out_shape=(
            jax.ShapeDtypeStruct((ROWS_DEV, 3, 2 * CH, U), bf16),
            jax.ShapeDtypeStruct((24, U), f32),
            jax.ShapeDtypeStruct((2 * NBLK - 1, BLK, BLK), bf16),
        ),
        in_specs=[hbm] + [vmem] * 7,
        out_specs=(vmem,) * 3,
        scratch_shapes=work + [pltpu.SemaphoreType.DMA],
        compiler_params=pltpu.CompilerParams(vmem_limit_bytes=24 * MIB),
        name="near_kernel",
    )(in_hbm(ramp_tiles()), own, near, w1, w2, w3, col1, col2)
    new_dual, send = pl.pallas_call(
        far_kernel,
        out_shape=(
            jax.ShapeDtypeStruct((ANG_DEV, ROWS_DEV, U), bf16),
            jax.ShapeDtypeStruct((BLOCKS, 4, LANES), f32),
        ),
        in_specs=[vmem] * 11,
        out_specs=(hbm, vmem),
        scratch_shapes=work + [
            pltpu.VMEM((ANG_DEV, ROWS_DEV, U), bf16),
            pltpu.SemaphoreType.DMA,
        ],
        compiler_params=pltpu.CompilerParams(vmem_limit_bytes=24 * MIB),
        name="far_kernel",
    )(angles, own, far, shared, taps, ramp, w1, w2, w3, col1, col2)
    got = lax.all_to_all(send, "ang", 0, 0, tiled=True)
    placed = pl.pallas_call(
        place_kernel,
        out_shape=jax.ShapeDtypeStruct((SLABS_DEV * ROW_DEVS * SLAB_Z, LANES), f32),
        in_specs=[vmem, vmem],
        out_specs=vmem,
        compiler_params=pltpu.CompilerParams(vmem_limit_bytes=4 * MIB),
        name="place_kernel",
    )(pick, got.reshape(4 * BLOCKS, LANES))
    shares = lax.all_to_all(placed.reshape(ROW_DEVS, SLABS_DEV * SLAB_Z, LANES), "row", 0, 0, tiled=True)
    return new_dual, jnp.sum(shares, axis=0)


def solution(mesh):
    field = P("ang", "row", None)
    return jax.shard_map(
        per_device,
        mesh=mesh,
        in_specs=(field, field, field) + (P(),) * 5 + (P("ang"),) * 3 + (P(), P()),
        out_specs=(field, P("row", "ang")),
        check_vma=False,
    )
```

```python
import math

import jax
import jax.numpy as jnp
import numpy as np
from jax import lax
from jax.experimental import pallas as pl
from jax.experimental.pallas import tpu as pltpu
from jax.sharding import PartitionSpec as P

U = 2048
CH = 32
ANG_DEV = 4
ROWS_DEV = 2
HALO = 3
FIELDS = 3
SLAB_Z = 4
SLABS_DEV = 4
BLOCKS = 16
ROW_DEVS = 16
LANES = 128
TILES = U // LANES
BLK = 256
NBLK = U // BLK
SPAN = ANG_DEV + 2 * HALO
ROWS1 = ROWS_DEV * (SPAN - 2) * CH
HALF1 = (SPAN - 2) * CH
GROUP1 = 5 * CH
GROUP2 = 3 * CH
OUT8 = ANG_DEV * ROWS_DEV
CENTRE = (U - 1) / 2.0
MIB = 1024 * 1024
MAG_LOW, MAG_HIGH, SHIFT_MAX = 0.85, 0.95, 8.0


def ramp_tiles():
    row_ids = np.arange(BLK, dtype=np.int32)[None, :, None]
    col_ids = np.arange(BLK, dtype=np.int32)[None, None, :]
    gaps = np.arange(-(NBLK - 1), NBLK, dtype=np.int32)[:, None, None] * BLK
    diff = row_ids - (col_ids + gaps)
    odd = np.abs(diff) % 2 == 1
    distance = np.where(odd, diff, 1).astype(np.float32)
    falloff = np.float32(-1.0) / (np.float32(math.pi * math.pi) * distance * distance)
    tiles = np.where(diff == 0, np.float32(0.25), np.where(odd, falloff, np.float32(0.0)))
    return jnp.asarray(tiles.astype(np.float32)).astype(jnp.bfloat16)


def shifted(value, step):
    lane = lax.broadcasted_iota(jnp.int32, value.shape, 1)
    if step < 0:
        return jnp.where(lane == 0, 0.0, pltpu.roll(value, 1, 1))
    return jnp.where(lane == U - 1, 0.0, pltpu.roll(value, U - 1, 1))


def silu(value):
    half = 0.5 * value
    return half + half * jnp.tanh(half)


def source_tiles(tile):
    ends = []
    for column in (tile * LANES, tile * LANES + LANES - 1):
        for mag in (MAG_LOW, MAG_HIGH):
            for shift in (-SHIFT_MAX, SHIFT_MAX):
                ends.append((column - CENTRE) * mag + CENTRE + shift)
    low = int(math.floor(min(ends) - 0.5))
    high = int(math.floor(max(ends) + 0.5)) + 1
    return max(low, 0) // LANES, min(high, U - 1) // LANES


def parity():
    return lax.axis_index("ang") % 2


def turned(index, last):
    return index + parity() * (last - 2 * index)


def pack_kernel(dual_hbm, forw_hbm, sino_hbm, own_ref, sems):
    loads = []
    for at, field in enumerate((dual_hbm, forw_hbm, sino_hbm)):
        loads.append(pltpu.make_async_copy(field, own_ref.at[pl.ds(at * ANG_DEV, ANG_DEV)], sems.at[at]))
    for load in loads:
        load.start()
    for load in loads:
        load.wait()


def layout_kernel(
    first_ref, middle_ref, last_ref, bias1_ref, bias2_ref, order_ref, offs_ref, mag_ref, move_ref, frac_ref,
    w1_ref, w2_ref, w3_ref, col1_ref, col2_ref, pick_ref, angle_ref,
    gather1, base2,
):
    f32, bf16 = jnp.float32, jnp.bfloat16
    gather1[...] = jnp.zeros(gather1.shape, f32)
    for ang_tap in range(3):
        for tap in range(3):
            part = 3 * ang_tap + tap
            gather1[3 * part:3 * part + 3, 0:CH] = first_ref[3 * turned(ang_tap, 2) + tap].astype(f32)
    key = lax.broadcasted_iota(jnp.int32, (32, 256), 0)
    lane = lax.broadcasted_iota(jnp.int32, (32, 256), 1)
    wanted = (key // 3 % 3) * 64 + (key % 3) * (2 * SPAN) + (key // 9) * 2
    spread = jnp.where((lane == wanted) & (key < 27), 1.0, 0.0)
    base1 = lax.dot_general(
        gather1[...].astype(bf16), spread.astype(bf16), (((0,), (0,)), ((), ())), preferred_element_type=f32
    )[0:CH]
    for row in range(ROWS_DEV):
        for ang in range(SPAN - 2):
            shift = 2 * ang + row
            rolled = pltpu.roll(base1, shift, 1) if shift else base1
            start = (row * (SPAN - 2) + ang) * CH
            w1_ref[start:start + CH, :] = rolled[:, 0:192].astype(bf16)
    base2[...] = jnp.zeros(base2.shape, f32)
    for ang_tap in range(3):
        for tap in range(3):
            block = middle_ref[3 * turned(ang_tap, 2) + tap].astype(f32)
            for ang in range(3):
                start = tap * GROUP1 + (ang + ang_tap) * CH
                base2[ang * CH:(ang + 1) * CH, start:start + CH] = block
    w2_ref[...] = base2[...].astype(bf16)
    w3_ref[...] = jnp.zeros(w3_ref.shape, f32)
    for ang_tap in range(3):
        block = last_ref[turned(ang_tap, 2)].astype(f32)
        for ang in range(ANG_DEV):
            source = ang + ang_tap
            for row in range(ROWS_DEV):
                start = row * GROUP2 + source % 3 * CH
                for tap in range(3):
                    at = tap * OUT8 + ang * ROWS_DEV + row
                    w3_ref[source // 3, at:at + 1, start:start + CH] = block[tap:tap + 1, :]
    square = (CH, CH)
    eye = lax.broadcasted_iota(jnp.int32, square, 0) == lax.broadcasted_iota(jnp.int32, square, 1)
    for bias_ref, col_ref in ((bias1_ref, col1_ref), (bias2_ref, col2_ref)):
        column = jnp.sum(jnp.where(eye, jnp.broadcast_to(bias_ref[...], square), 0.0), axis=1, keepdims=True)
        col_ref[...] = jnp.broadcast_to(column, (CH, LANES))
    ang = lax.broadcasted_iota(jnp.int32, (OUT8, ANG_DEV), 0) // ROWS_DEV
    mine = lax.broadcasted_iota(jnp.int32, (OUT8, ANG_DEV), 1) == turned(ang, ANG_DEV - 1)
    for at, ref in enumerate((mag_ref, move_ref, frac_ref)):
        value = jnp.sum(jnp.where(mine, jnp.broadcast_to(ref[...], (OUT8, ANG_DEV)), 0.0), axis=1, keepdims=True)
        angle_ref[at] = jnp.broadcast_to(value, (OUT8, LANES))
    slabs = SLABS_DEV * ROW_DEVS
    chosen = jnp.broadcast_to(order_ref[...], (slabs, slabs)) == lax.broadcasted_iota(jnp.int32, (slabs, slabs), 0)
    chosen = jnp.where(chosen, 1.0, 0.0).astype(bf16)
    starts = jnp.dot(offs_ref[...].astype(f32).astype(bf16), chosen, preferred_element_type=f32)
    width = 3 * 4 * BLOCKS
    block_of = (lax.broadcasted_iota(jnp.int32, (BLOCKS, width), 1) % (4 * BLOCKS)) // 4
    widen = jnp.where(block_of == lax.broadcasted_iota(jnp.int32, (BLOCKS, width), 0), 1.0, 0.0).astype(bf16)
    starts = lax.dot_general(
        starts.astype(bf16), widen, (((0,), (0,)), ((), ())), preferred_element_type=f32
    )
    rows = slabs * SLAB_Z
    slot_of = lax.broadcasted_iota(jnp.int32, (rows, slabs), 0) // SLAB_Z
    tall = jnp.where(slot_of == lax.broadcasted_iota(jnp.int32, (rows, slabs), 1), 1.0, 0.0).astype(bf16)
    starts = jnp.dot(tall, starts.astype(bf16), preferred_element_type=f32)
    depth = lax.broadcasted_iota(jnp.int32, (rows, width), 0) % SLAB_Z
    kind = lax.broadcasted_iota(jnp.int32, (rows, width), 1) % 4
    offset = depth + kind // 2 - kind % 2 - ROWS_DEV * lax.axis_index("row")
    pick_ref[...] = jnp.where(starts + offset.astype(f32) == 0.0, 0.125, 0.0).astype(bf16)


def lay_inputs(x32, xcat, own_ref, side_ref, side, skip):
    f32, bf16 = jnp.float32, jnp.bfloat16
    x32[...] = jnp.zeros(x32.shape, f32)
    for field in range(FIELDS):
        base = field * 2 * SPAN
        for ang in range(ANG_DEV):
            at = base + 2 * (HALO + ang)
            x32[at:at + 2, :] = own_ref[field * ANG_DEV + turned(ang, ANG_DEV - 1)].astype(f32)
        for ang in range(HALO):
            at = base + 2 * (side + ang)
            x32[at:at + 2, :] = side_ref[field * ANG_DEV + turned(skip + ang, ANG_DEV - 1)].astype(f32)
    stacked = x32[...]
    xcat[0:64, :] = shifted(stacked, -1).astype(bf16)
    xcat[64:128, :] = stacked.astype(bf16)
    xcat[128:192, :] = shifted(stacked, 1).astype(bf16)


def first_layer(xcat, w1_ref, bias1, act1, row, first, count):
    f32, bf16 = jnp.float32, jnp.bfloat16
    start, size = row * HALF1 + first * CH, count * CH
    lane = lax.broadcasted_iota(jnp.int32, (size, LANES), 1)
    nothing = jnp.zeros((size, LANES), bf16)
    before_edge, after_rest = nothing, None
    for step in range(NBLK):
        cols = slice(step * BLK, (step + 1) * BLK)
        block = jnp.dot(w1_ref[start:start + size, :], xcat[:, cols], preferred_element_type=f32)
        act = jnp.concatenate(
            [silu(block[part * CH:(part + 1) * CH] + bias1) for part in range(count)], axis=0
        ).astype(bf16)
        act1[row, GROUP1:GROUP1 + size, cols] = act
        before = pltpu.roll(act, 1, 1)
        act1[row, 0:size, step * BLK:step * BLK + LANES] = jnp.where(lane == 0, before_edge, before[:, 0:LANES])
        act1[row, 0:size, step * BLK + LANES:(step + 1) * BLK] = before[:, LANES:]
        before_edge = before[:, 0:LANES]
        after = pltpu.roll(act, BLK - 1, 1)
        act1[row, 2 * GROUP1:2 * GROUP1 + size, step * BLK:step * BLK + LANES] = after[:, 0:LANES]
        if step:
            act1[row, 2 * GROUP1:2 * GROUP1 + size, step * BLK - LANES:step * BLK] = jnp.where(
                lane == LANES - 1, after[:, LANES:], after_rest
            )
        after_rest = after[:, LANES:]
    act1[row, 2 * GROUP1:2 * GROUP1 + size, U - LANES:] = jnp.where(lane == LANES - 1, nothing, after_rest)


def first_layer_whole(xcat, w1_ref, bias1, act1, row, first, count):
    f32, bf16 = jnp.float32, jnp.bfloat16
    start = row * HALF1 + first * CH
    for step in range(NBLK):
        cols = slice(step * BLK, (step + 1) * BLK)
        block = jnp.dot(w1_ref[start:start + count * CH, :], xcat[:, cols], preferred_element_type=f32)
        for part in range(count):
            rows = slice(GROUP1 + part * CH, GROUP1 + (part + 1) * CH)
            act1[row, rows, cols] = silu(block[part * CH:(part + 1) * CH] + bias1).astype(bf16)
    edge = lax.broadcasted_iota(jnp.int32, (CH, LANES), 1)
    for part in range(count):
        low, middle, high = (slice(tap * GROUP1 + part * CH, tap * GROUP1 + (part + 1) * CH) for tap in range(3))
        here = act1[row, middle, :]
        before = pltpu.roll(here, 1, 1)
        after = pltpu.roll(here, U - 1, 1)
        act1[row, low, LANES:] = before[:, LANES:]
        act1[row, low, 0:LANES] = jnp.where(edge == 0, 0.0, before[:, 0:LANES].astype(f32)).astype(bf16)
        act1[row, high, 0:U - LANES] = after[:, 0:U - LANES]
        last = after[:, U - LANES:].astype(f32)
        act1[row, high, U - LANES:] = jnp.where(edge == LANES - 1, 0.0, last).astype(bf16)


def second_layer(w2_ref, bias2, act1, act2):
    f32, bf16 = jnp.float32, jnp.bfloat16
    for row in range(ROWS_DEV):
        for step in range(NBLK):
            cols = slice(step * BLK, (step + 1) * BLK)
            block = jnp.dot(w2_ref[...], act1[row, :, cols], preferred_element_type=f32)
            for part in range(3):
                rows = slice(row * GROUP2 + part * CH, row * GROUP2 + (part + 1) * CH)
                act2[rows, cols] = silu(block[part * CH:(part + 1) * CH] + bias2).astype(bf16)


def near_kernel(
    ramp_hbm, own_ref, near_ref, w1_ref, w2_ref, w3_ref, col1_ref, col2_ref,
    shared_ref, taps_ref, ramp_ref,
    x32, xcat, act1, act2, sem,
):
    load = pltpu.make_async_copy(ramp_hbm, ramp_ref, sem)
    load.start()
    bias1, bias2 = col1_ref[:, 0:1], col2_ref[:, 0:1]
    lay_inputs(x32, xcat, own_ref, near_ref, HALO + ANG_DEV, 0)
    for row in range(ROWS_DEV):
        first_layer_whole(xcat, w1_ref, bias1, act1, row, 3, 5)
        for tap in range(3):
            shared_ref[row, tap] = act1[row, tap * GROUP1:tap * GROUP1 + 2 * CH, :]
    second_layer(w2_ref, bias2, act1, act2)
    taps_ref[...] = jnp.dot(w3_ref[1].astype(jnp.bfloat16), act2[...], preferred_element_type=jnp.float32)
    load.wait()


def far_kernel(
    angle_ref, own_ref, far_ref, shared_ref, taps_ref, ramp_ref,
    w1_ref, w2_ref, w3_ref, col1_ref, col2_ref,
    dual_hbm, send_ref,
    x32, xcat, act1, act2, dual_ref, sem,
):
    f32, bf16 = jnp.float32, jnp.bfloat16
    bias1, bias2 = col1_ref[:, 0:1], col2_ref[:, 0:1]
    lay_inputs(x32, xcat, own_ref, far_ref, 0, 1)
    for row in range(ROWS_DEV):
        first_layer(xcat, w1_ref, bias1, act1, row, 0, 3)
        for tap in range(3):
            act1[row, tap * GROUP1 + 3 * CH:(tap + 1) * GROUP1, :] = shared_ref[row, tap]
    second_layer(w2_ref, bias2, act1, act2)
    taps3 = taps_ref[...] + jnp.dot(w3_ref[0].astype(bf16), act2[...], preferred_element_type=f32)
    update = shifted(taps3[0:8], -1) + taps3[8:16] + shifted(taps3[16:24], 1)
    own_dual = x32[2 * HALO:2 * HALO + OUT8, :]
    new_dual = (own_dual + update).astype(bf16)
    for ang in range(ANG_DEV):
        dual_ref[turned(ang, ANG_DEV - 1)] = new_dual[2 * ang:2 * ang + 2, :]
    store = pltpu.make_async_copy(dual_ref, dual_hbm, sem)
    store.start()
    dual32 = new_dual.astype(f32)
    blocks = jnp.concatenate([dual32[:, b * BLK:(b + 1) * BLK] for b in range(NBLK)], axis=0).astype(bf16)
    filtered = [None] * NBLK
    for gap in range(-(NBLK - 1), NBLK):
        part = jnp.dot(blocks, ramp_ref[gap + NBLK - 1], preferred_element_type=f32)
        for source in range(NBLK):
            target = source + gap
            if 0 <= target < NBLK:
                piece = part[source * OUT8:(source + 1) * OUT8]
                filtered[target] = piece if filtered[target] is None else filtered[target] + piece
    lanes = [filtered[t // 2][:, (t % 2) * LANES:(t % 2 + 1) * LANES] for t in range(TILES)]
    row_id = lax.broadcasted_iota(jnp.int32, (OUT8, LANES), 0)
    lane_id = lax.broadcasted_iota(jnp.int32, (OUT8, LANES), 1)
    mag, move, frac = angle_ref[0], angle_ref[1], angle_ref[2]
    keep = 1.0 - frac
    for tile in range(TILES):
        column = (lane_id + tile * LANES).astype(f32)
        place = (column - CENTRE) * mag + CENTRE + move
        floor = jnp.floor(place)
        weight = place - floor
        low = floor.astype(jnp.int32)
        high = low + 1
        first, last = source_tiles(tile)
        left = jnp.zeros((OUT8, LANES), f32)
        right = jnp.zeros((OUT8, LANES), f32)
        for source in range(first, last + 1):
            got = jnp.take_along_axis(lanes[source], low & (LANES - 1), axis=1, mode="promise_in_bounds")
            left = jnp.where(low // LANES == source, got, left)
            got = jnp.take_along_axis(lanes[source], high & (LANES - 1), axis=1, mode="promise_in_bounds")
            right = jnp.where(high // LANES == source, got, right)
        projected = ((1.0 - weight) * left + weight * right).astype(bf16).astype(f32)
        lower = keep * projected
        upper = frac * projected
        lower = lower + pltpu.roll(lower, 4, 0)
        lower = lower + pltpu.roll(lower, 2, 0)
        upper = upper + pltpu.roll(upper, 4, 0)
        upper = upper + pltpu.roll(upper, 2, 0)
        packed = jnp.where(row_id < ROWS_DEV, lower, upper)
        send_ref[tile] = packed[0:4]
    store.wait()


def place_kernel(pick_ref, got_ref, out_ref):
    f32, bf16 = jnp.float32, jnp.bfloat16
    rows = got_ref[...]
    high = rows.astype(bf16)
    rest = rows - high.astype(f32)
    mid = rest.astype(bf16)
    low = (rest - mid.astype(f32)).astype(bf16)
    parts = jnp.concatenate([high, mid, low], axis=0)
    out_ref[...] = jnp.dot(pick_ref[...], parts, preferred_element_type=f32)


def in_hbm(value):
    return pltpu.with_memory_space_constraint(value, pltpu.HBM)


def per_device(
    dual_field, forward, sinogram, first_weight, first_bias, middle_weight, middle_bias, last_weight,
    magnify, detector_shift, row_fraction, offsets, slab_order,
):
    f32, bf16 = jnp.float32, jnp.bfloat16
    vmem = pl.BlockSpec(memory_space=pltpu.VMEM)
    hbm = pl.BlockSpec(memory_space=pltpu.HBM)
    own = pl.pallas_call(
        pack_kernel,
        out_shape=jax.ShapeDtypeStruct((FIELDS * ANG_DEV, ROWS_DEV, U), bf16),
        in_specs=[hbm] * 3,
        out_specs=vmem,
        scratch_shapes=[pltpu.SemaphoreType.DMA((3,))],
        compiler_params=pltpu.CompilerParams(vmem_limit_bytes=2 * MIB),
        name="pack_kernel",
    )(*map(in_hbm, (dual_field, forward, sinogram)))
    count = lax.axis_size("ang")
    near = lax.ppermute(own, "ang", [(i, i ^ 1) for i in range(count)])
    far = lax.ppermute(own, "ang", [(i, (i + 1 if i % 2 else i - 1) % count) for i in range(count)])
    width = 3 * 4 * BLOCKS
    w1, w2, w3, col1, col2, pick, angles = pl.pallas_call(
        layout_kernel,
        out_shape=(
            jax.ShapeDtypeStruct((ROWS1, 192), bf16),
            jax.ShapeDtypeStruct((GROUP2, 3 * GROUP1), bf16),
            jax.ShapeDtypeStruct((2, 24, 2 * GROUP2), f32),
            jax.ShapeDtypeStruct((CH, LANES), f32),
            jax.ShapeDtypeStruct((CH, LANES), f32),
            jax.ShapeDtypeStruct((SLABS_DEV * ROW_DEVS * SLAB_Z, width), bf16),
            jax.ShapeDtypeStruct((3, OUT8, LANES), f32),
        ),
        out_specs=(vmem,) * 7,
        scratch_shapes=[
            pltpu.VMEM((32, LANES), f32),
            pltpu.VMEM((GROUP2, 3 * GROUP1), f32),
        ],
        compiler_params=pltpu.CompilerParams(vmem_limit_bytes=8 * MIB),
        name="layout_kernel",
    )(*map(in_hbm, (
        first_weight.transpose(0, 1, 3, 2).reshape(9, FIELDS, CH), middle_weight.reshape(9, CH, CH),
        last_weight.transpose(0, 2, 1, 3).reshape(3, 3, CH), first_bias[None], middle_bias[None],
        slab_order[None], offsets, magnify[None], detector_shift[None], row_fraction[None],
    )))
    work = [
        pltpu.VMEM((64, U), f32),
        pltpu.VMEM((192, U), bf16),
        pltpu.VMEM((ROWS_DEV, 3 * GROUP1, U), bf16),
        pltpu.VMEM((ROWS_DEV * GROUP2, U), bf16),
    ]
    shared, taps, ramp = pl.pallas_call(
        near_kernel,
        out_shape=(
            jax.ShapeDtypeStruct((ROWS_DEV, 3, 2 * CH, U), bf16),
            jax.ShapeDtypeStruct((24, U), f32),
            jax.ShapeDtypeStruct((2 * NBLK - 1, BLK, BLK), bf16),
        ),
        in_specs=[hbm] + [vmem] * 7,
        out_specs=(vmem,) * 3,
        scratch_shapes=work + [pltpu.SemaphoreType.DMA],
        compiler_params=pltpu.CompilerParams(vmem_limit_bytes=24 * MIB),
        name="near_kernel",
    )(in_hbm(ramp_tiles()), own, near, w1, w2, w3, col1, col2)
    new_dual, send = pl.pallas_call(
        far_kernel,
        out_shape=(
            jax.ShapeDtypeStruct((ANG_DEV, ROWS_DEV, U), bf16),
            jax.ShapeDtypeStruct((BLOCKS, 4, LANES), f32),
        ),
        in_specs=[vmem] * 11,
        out_specs=(hbm, vmem),
        scratch_shapes=work + [
            pltpu.VMEM((ANG_DEV, ROWS_DEV, U), bf16),
            pltpu.SemaphoreType.DMA,
        ],
        compiler_params=pltpu.CompilerParams(vmem_limit_bytes=24 * MIB),
        name="far_kernel",
    )(angles, own, far, shared, taps, ramp, w1, w2, w3, col1, col2)
    got = lax.all_to_all(send, "ang", 0, 0, tiled=True)
    placed = pl.pallas_call(
        place_kernel,
        out_shape=jax.ShapeDtypeStruct((SLABS_DEV * ROW_DEVS * SLAB_Z, LANES), f32),
        in_specs=[vmem, vmem],
        out_specs=vmem,
        compiler_params=pltpu.CompilerParams(vmem_limit_bytes=4 * MIB),
        name="place_kernel",
    )(pick, got.reshape(4 * BLOCKS, LANES))
    shares = lax.all_to_all(placed.reshape(ROW_DEVS, SLABS_DEV * SLAB_Z, LANES), "row", 0, 0, tiled=True)
    return new_dual, jnp.sum(shares, axis=0)


def solution(mesh):
    field = P("ang", "row", None)
    return jax.shard_map(
        per_device,
        mesh=mesh,
        in_specs=(field, field, field) + (P(),) * 5 + (P("ang"),) * 3 + (P(), P()),
        out_specs=(field, P("row", "ang")),
        check_vma=False,
    )
```
